256 devices in a mesh: gx: 16 (over y_hi, x, core), gy: 16 (over y_lo, z).
Axes of the slice: x: 4, y: 4 (y_hi: 2, y_lo: 2; y = y_hi * 2 + y_lo), z: 8, core: 2. Of those that a mesh axis runs over, the one named last changes fastest.
Arguments:
- object_field: float32 [2, 8192, 8192], P(None, 'gy', 'gx'), may hold values from -6 to 6
- probe: float32 [3, 2, 256, 256], replicated, may hold values from -6 to 6
- positions: int32 [16, 16, 4, 2], P('gy', 'gx'), may hold values from 0 to 512
- frame_count: int32 [16, 16], P('gy', 'gx'), may hold values from 1 to 4, as said below
- measured: float32 [16, 16, 4, 256, 256], P('gy', 'gx'), may hold values from 0.5 to 20
Outputs:
- object_grad: float32 [2, 8192, 8192], P(None, 'gy', 'gx')
The draws below stay inside these ranges and needn't reach their ends.
Inputs may be any that keep to these rules, and one draw needn't show every extreme that they name: `frame_count`: some tile has all 4 slots live in every draw; live frames fill the first slots of a tile; tiles in the columns tx >= 8 have exactly 1 live frame.
All inputs are finite; a program needn't handle non-finite values.
Results may differ from the reference program's by a relative error of at most 0.0045.
Values sent between devices are 32-bit elements; how exact they have to be, the bound alone decides.
A program may use at most 64 MiB of HBM per device.

```python
import math
import jax
import jax.numpy as jnp
from jax import lax

W = 256
MODES = 3
TILE = 512
HALO = 128
SLOTS = 4
NR = 8192
NC = 8192
N_GX = 16
N_GY = 16


def draw_frame_count(key, part):
    first, second, third, fourth = jax.random.split(jax.random.fold_in(key, 17), 4)
    light = jax.random.randint(first, (N_GY, N_GX), 1, SLOTS // 2 + 1)
    heavy = jax.random.randint(second, (N_GY, N_GX), 0, 2) == 0
    sparse = jax.random.randint(fourth, (N_GY, N_GX), 1, SLOTS // 4 + 1)
    column = jnp.arange(N_GX, dtype=jnp.int32)[None, :]
    left_side = column < N_GX // 2
    counted = jnp.where(left_side, jnp.where(heavy, SLOTS, light), sparse)
    chosen_row = jax.random.randint(third, (), 0, N_GY)
    chosen_col = jax.random.randint(jax.random.fold_in(third, 5), (), 0, N_GX // 2)
    counted = counted.at[chosen_row, chosen_col].set(SLOTS)
    return counted.astype(jnp.int32)


def with_ends(entries, key, least, top_value):
    extent = entries.shape
    spot = [jax.random.randint(jax.random.fold_in(key, axis), (), 0, extent[axis]) for axis in range(len(extent))]
    entries = entries.at[tuple(spot)].set(least)
    longest = extent.index(max(extent))
    spot[longest] = (spot[longest] + 1) % extent[longest]
    return entries.at[tuple(spot)].set(top_value)


def shard_levels(stream_key, dims, pieces, least, top_value):
    loudness = 1.0
    for position, blocks in pieces:
        draws = jax.random.uniform(jax.random.fold_in(jax.random.fold_in(stream_key, 6), position), (blocks,), jnp.float32, least / len(pieces), top_value / len(pieces))
        loudness = loudness * jnp.repeat(jnp.exp(draws), dims[position] // blocks).reshape((-1,) + (1,) * (len(dims) - 1 - position))
    return loudness


def scatter_about(rng, dims, spread, limit, cuts=(), kind=jnp.bfloat16):
    array = jax.random.normal(rng, dims, jnp.float32) * spread
    if len(cuts) > 0:
        array = shard_levels(rng, dims, cuts, -0.22, 0.18) * array
    return jnp.clip(array, min=-limit, max=limit).astype(kind)


def setup_inputs(seed: int = 0) -> dict:
    splits = jax.random.split(jax.random.key(seed), 6)
    return {
        "object_field": scatter_about(splits[0], (2, NR, NC), 1.0, 6.0, ((1, 16), (2, 16)), jnp.float32),
        "probe": scatter_about(splits[1], (MODES, 2, W, W), 1.0, 6.0, (), jnp.float32),
        "positions": with_ends(jax.random.randint(splits[2], (N_GY, N_GX, SLOTS, 2), 0, TILE - W + 2 * HALO + 1), jax.random.fold_in(splits[2], 1), 0, TILE - W + 2 * HALO).astype(jnp.int32),
        "frame_count": draw_frame_count(jax.random.fold_in(splits[5], 71), 0),
        "measured": jnp.clip(jnp.exp(math.log(20.0) - 3.6888795 * jax.random.uniform(splits[4], (N_GY, N_GX, SLOTS, W, W), jnp.float32) ** shard_levels(splits[4], (N_GY, N_GX, SLOTS, W, W), ((0, 16), (1, 16)), -0.2, 0.2)), 0.5, 20.0),
    }


def dft_table(width, sign):
    index = jnp.arange(width, dtype=jnp.float32)
    phase = 2.0 * math.pi / width * jnp.mod(jnp.outer(index, index), width)
    scale = 1.0 / math.sqrt(width)
    cosine = jnp.cos(phase) * scale
    imag_part = sign * jnp.sin(phase) * scale
    upper = jnp.concatenate([cosine, imag_part], axis=1)
    lower = jnp.concatenate([-imag_part, cosine], axis=1)
    return jnp.concatenate([upper, lower], axis=0).astype(jnp.bfloat16)

def apply_rows(real_part, imag_part, table):
    modes, rows, width = real_part.shape
    joined = jnp.concatenate([real_part, imag_part], axis=-1).reshape(modes * rows, 2 * width)
    result = jnp.dot(joined, table, preferred_element_type=jnp.float32).reshape(modes, rows, 2 * width)
    return (result[..., :width], result[..., width:])

def frame_grad(patch, probe, measure, forward, inverse):
    probe_re = probe[:, 0]
    probe_im = probe[:, 1]
    psi_re = (probe_re * patch[0] - probe_im * patch[1]).astype(jnp.bfloat16)
    psi_im = (probe_re * patch[1] + probe_im * patch[0]).astype(jnp.bfloat16)
    half_re, half_im = apply_rows(psi_re, psi_im, forward)
    half_re = jnp.swapaxes(half_re.astype(jnp.bfloat16), 1, 2)
    half_im = jnp.swapaxes(half_im.astype(jnp.bfloat16), 1, 2)
    wave_re, wave_im = apply_rows(half_re, half_im, forward)
    inten = lax.optimization_barrier(jnp.sum(wave_re * wave_re + wave_im * wave_im, axis=0))
    factor = 1.0 - jnp.sqrt(measure).T / jnp.sqrt(inten + 1.0)
    resid_re = (factor * wave_re).astype(jnp.bfloat16)
    resid_im = (factor * wave_im).astype(jnp.bfloat16)
    back_re, back_im = apply_rows(resid_re, resid_im, inverse)
    back_re = jnp.swapaxes(back_re.astype(jnp.bfloat16), 1, 2)
    back_im = jnp.swapaxes(back_im.astype(jnp.bfloat16), 1, 2)
    chi_re, chi_im = apply_rows(back_re, back_im, inverse)
    grad_re = lax.optimization_barrier(jnp.sum(probe_re * chi_re + probe_im * chi_im, axis=0))
    grad_im = lax.optimization_barrier(jnp.sum(probe_re * chi_im - probe_im * chi_re, axis=0))
    return jnp.stack([grad_re, grad_im])

def reference(object_field, probe, positions, frame_count, measured):
    forward = dft_table(W, -1.0)
    inverse = dft_table(W, 1.0)
    padded = jnp.pad(object_field, ((0, 0), (HALO, HALO), (HALO, HALO)))
    zero = jnp.zeros((), jnp.int32)

    def one_tile(index, total):
        row_tile = (index // N_GX).astype(jnp.int32)
        col_tile = (index % N_GX).astype(jnp.int32)
        spots = positions[row_tile, col_tile]
        frames = measured[row_tile, col_tile]

        def one_frame(slot, acc):
            row = (row_tile * TILE + spots[slot, 0]).astype(jnp.int32)
            col = (col_tile * TILE + spots[slot, 1]).astype(jnp.int32)
            patch = lax.dynamic_slice(padded, (zero, row, col), (2, W, W))
            grad = frame_grad(patch, probe, frames[slot], forward, inverse)
            old = lax.dynamic_slice(acc, (zero, row, col), (2, W, W))
            return lax.dynamic_update_slice(acc, old + grad, (zero, row, col))
        return lax.fori_loop(0, frame_count[row_tile, col_tile], one_frame, total)
    total = lax.fori_loop(0, N_GY * N_GX, one_tile, jnp.zeros_like(padded))
    return total[:, HALO:HALO + NR, HALO:HALO + NC]
```

```python
import functools
import math

import jax
import jax.numpy as jnp
import ml_dtypes
import numpy as np
from jax import lax
from jax.experimental import pallas as pl
from jax.experimental.pallas import tpu as pltpu
from jax.sharding import PartitionSpec as P

HALO = 128
W = 256
H = 128
LANES = 128
F32 = jnp.float32
BF16 = jnp.bfloat16


def dft_tables():
    j = np.arange(H)[:, None]
    k = np.arange(H)[None, :]
    tables = []
    for odd in (0, 1):
        phase = 2.0 * math.pi / W * np.mod(j * (2 * k + odd), W)
        cosine = np.cos(phase) / math.sqrt(W)
        sine = np.sin(phase) / math.sqrt(W)
        tables.append(np.block([[cosine, -sine], [sine, cosine]]))
    tables += [tables[0].T, tables[1].T]
    return np.stack(tables).astype(ml_dtypes.bfloat16)


def dot(a, b):
    return jnp.dot(a, b, preferred_element_type=F32)


def frames_kernel(
    spots, count, tables, probe, root, own, above, below, before, after,
    total_out,
    ext, total, patch, stage2, wave, stage3, stage4, grad, sem,
):
    modes = probe.shape[0]
    tile = own.shape[1]
    side = tile + 2 * HALO
    copies = []

    def load(source, rows, first):
        for i in range(source.shape[2] // LANES):
            n = len(copies)
            copy = pltpu.make_async_copy(source.at[:, :, pl.ds(i * LANES, LANES)], ext.at[:, first + i, rows, :], sem.at[n])
            copy.start()
            copies.append(copy)

    load(own, pl.ds(HALO, tile), 1)
    load(above, pl.ds(0, HALO), 1)
    load(below, pl.ds(HALO + tile, HALO), 1)
    load(before, pl.ds(0, side), 0)
    load(after, pl.ds(0, side), 1 + tile // LANES)

    @pl.loop(0, side // 16)
    def _(i):
        total[:, :, pl.ds(pl.multiple_of(i * 16, 16), 16), :] = jnp.zeros((2, total.shape[1], 16, LANES), F32)

    for copy in copies:
        copy.wait()

    lane = lax.broadcasted_iota(jnp.int32, (W, LANES), 1)

    @pl.loop(0, count[0, 0])
    def _(slot):
        row = spots[slot, 0]
        column = spots[slot, 1]
        block = column // LANES
        shift = column - block * LANES
        back = lax.rem(LANES - shift, LANES)
        keep = lane < LANES - shift
        for part in range(2):
            rolled = []
            for i in range(3):
                x = ext[part, block + i, pl.ds(row, W), :]
                rolled.append(pltpu.roll(x, back, axis=1))
            for i in range(2):
                patch[part, :, i * LANES:(i + 1) * LANES] = jnp.where(keep, rolled[i], rolled[i + 1])

        step = 32
        @pl.loop(0, H // step)
        def _(i):
            first = pl.multiple_of(i * step, step)
            even, odd = [], []
            for m in range(modes):
                for half in range(2):
                    rows = pl.ds(half * H + first, step)
                    pr, pi = probe[m, 0, rows, :], probe[m, 1, rows, :]
                    xr, xi = patch[0, rows, :], patch[1, rows, :]
                    re = pr * xr - pi * xi
                    im = pr * xi + pi * xr
                    even.append(jnp.concatenate([re[:, :H] + re[:, H:], im[:, :H] + im[:, H:]], axis=1))
                    odd.append(jnp.concatenate([re[:, :H] - re[:, H:], im[:, :H] - im[:, H:]], axis=1))
            even = dot(jnp.concatenate(even, axis=0).astype(BF16), tables[0])
            odd = dot(jnp.concatenate(odd, axis=0).astype(BF16), tables[1])
            for m in range(modes):
                for n, h in enumerate((even, odd)):
                    low = h[(2 * m) * step:(2 * m + 1) * step]
                    high = h[(2 * m + 1) * step:(2 * m + 2) * step]
                    plus, minus = (low + high).astype(BF16), (low - high).astype(BF16)
                    for part in range(2):
                        rows = pl.ds(part * H + first, step)
                        columns = slice(part * H, (part + 1) * H)
                        stage2[m, 0, rows, n * H:(n + 1) * H] = plus[:, columns]
                        stage2[m, 1, rows, n * H:(n + 1) * H] = minus[:, columns]

        for m in range(modes):
            for n in range(2):
                wave[m, n] = dot(tables[2 + n], stage2[m, n])

        for n in range(2):
            @pl.loop(0, H // 16)
            def _(i):
                first = pl.multiple_of(i * 16, 16)
                res = [wave[m, n, pl.ds(first, 16), :] for m in range(modes)]
                ims = [wave[m, n, pl.ds(H + first, 16), :] for m in range(modes)]
                inten = sum(x * x for x in res) + sum(x * x for x in ims)
                factor = 1.0 - root[slot, pl.ds(n * H + first, 16), :] / jnp.sqrt(inten + 1.0)
                for m in range(modes):
                    stage3[m, n, pl.ds(first, 16), :] = (factor * res[m]).astype(BF16)
                    stage3[m, n, pl.ds(H + first, 16), :] = (factor * ims[m]).astype(BF16)

        for m in range(modes):
            even = dot(tables[0], stage3[m, 0])
            odd = dot(tables[1], stage3[m, 1])
            plus, minus = (even + odd).astype(BF16), (even - odd).astype(BF16)
            for half, x in enumerate((plus, minus)):
                for part in range(2):
                    for n in range(2):
                        stage4[n, m, half * H:(half + 1) * H, part * H:(part + 1) * H] = x[part * H:(part + 1) * H, n * H:(n + 1) * H]

        @pl.loop(0, W // step)
        def _(i):
            rows = pl.ds(pl.multiple_of(i * step, step), step)
            even = dot(stage4[0, :, rows, :].reshape(modes * step, W), tables[2])
            odd = dot(stage4[1, :, rows, :].reshape(modes * step, W), tables[3])
            plus, minus = even + odd, even - odd
            for half, x in enumerate((plus, minus)):
                columns = slice(half * H, (half + 1) * H)
                gr = gi = 0.0
                for m in range(modes):
                    pr, pi = probe[m, 0, rows, columns], probe[m, 1, rows, columns]
                    cr, ci = x[m * step:(m + 1) * step, :H], x[m * step:(m + 1) * step, H:]
                    gr = gr + (pr * cr + pi * ci)
                    gi = gi + (pr * ci - pi * cr)
                grad[0, rows, columns] = gr
                grad[1, rows, columns] = gi

        moved = lane >= shift
        for part in range(2):
            left = pltpu.roll(grad[part, :, 0:LANES], shift, axis=1)
            right = pltpu.roll(grad[part, :, LANES:2 * LANES], shift, axis=1)
            zero = jnp.zeros_like(left)
            pieces = (jnp.where(moved, left, zero), jnp.where(moved, right, left), jnp.where(moved, zero, right))
            for i, piece in enumerate(pieces):
                where = (part, block + i, pl.ds(row, W), slice(None))
                total[where] = total[where] + piece

    copies = [
        pltpu.make_async_copy(total.at[:, i], total_out.at[:, :, pl.ds(i * LANES, LANES)], sem.at[i])
        for i in range(side // LANES)
    ]
    for copy in copies:
        copy.start()
    for copy in copies:
        copy.wait()


def frames_call(spots, count, probe, root, own, above, below, before, after):
    modes = probe.shape[0]
    side = own.shape[1] + 2 * HALO
    wide = side + LANES
    smem = pl.BlockSpec(memory_space=pltpu.SMEM)
    vmem = pl.BlockSpec(memory_space=pltpu.VMEM)
    hbm = pl.BlockSpec(memory_space=pl.ANY)
    return pl.pallas_call(
        frames_kernel,
        out_shape=jax.ShapeDtypeStruct((2, side, side), F32),
        in_specs=[smem, smem, vmem, vmem, vmem, hbm, hbm, hbm, hbm, hbm],
        out_specs=hbm,
        scratch_shapes=[
            pltpu.VMEM((2, wide // LANES, side, LANES), F32),
            pltpu.VMEM((2, wide // LANES, side, LANES), F32),
            pltpu.VMEM((2, W, W), F32),
            pltpu.VMEM((modes, 2, W, W), BF16),
            pltpu.VMEM((modes, 2, W, W), F32),
            pltpu.VMEM((modes, 2, W, W), BF16),
            pltpu.VMEM((2, modes, W, W), BF16),
            pltpu.VMEM((2, W, W), F32),
            pltpu.SemaphoreType.DMA((16,)),
        ],
        compiler_params=pltpu.CompilerParams(vmem_limit_bytes=60 * 1024 * 1024),
        name="frames",
    )(spots, count, jnp.asarray(dft_tables()), probe, root, own, above, below, before, after)


def passed_along(array, axis, by):
    devices = lax.axis_size(axis)
    pairs = [(i, i + by) for i in range(devices) if 0 <= i + by < devices]
    return lax.ppermute(array, axis, pairs)


def body(object_field, probe, positions, frame_count, measured):
    border = HALO
    spots = positions[0, 0]
    count = frame_count
    root = jnp.sqrt(measured[0, 0])
    slots = root.shape[0]
    root = root.reshape(slots, H, 2, H, 2).transpose(0, 2, 1, 4, 3).reshape(slots, W, W)
    above = passed_along(object_field[:, -border:, :], "gy", 1)
    below = passed_along(object_field[:, :border, :], "gy", -1)
    left = jnp.concatenate([x[:, :, :border] for x in (above, object_field, below)], axis=1)
    right = jnp.concatenate([x[:, :, -border:] for x in (above, object_field, below)], axis=1)
    before = passed_along(right, "gx", 1)
    after = passed_along(left, "gx", -1)

    total = frames_call(spots, count, probe, root, object_field, above, below, before, after)

    upper_rim = total[:, :border, :]
    lower_rim = total[:, -border:, :]
    from_below = passed_along(upper_rim, "gy", -1)
    from_above = passed_along(lower_rim, "gy", 1)
    middle = total[:, border:-border, :]
    middle = middle.at[:, -border:, :].add(from_below)
    middle = middle.at[:, :border, :].add(from_above)
    left_rim = middle[:, :, :border]
    right_rim = middle[:, :, -border:]
    from_right = passed_along(left_rim, "gx", -1)
    from_left = passed_along(right_rim, "gx", 1)
    inner = middle[:, :, border:-border]
    inner = inner.at[:, :, -border:].add(from_right)
    inner = inner.at[:, :, :border].add(from_left)
    return inner


def solution(mesh):
    return jax.shard_map(
        body,
        mesh=mesh,
        in_specs=(
            P(None, "gy", "gx"),
            P(),
            P("gy", "gx", None, None),
            P("gy", "gx"),
            P("gy", "gx", None, None, None),
        ),
        out_specs=P(None, "gy", "gx"),
        check_vma=False,
    )
```

```python
import functools
import math

import jax
import jax.numpy as jnp
import ml_dtypes
import numpy as np
from jax import lax
from jax.experimental import pallas as pl
from jax.experimental.pallas import tpu as pltpu
from jax.sharding import PartitionSpec as P

HALO = 128
W = 256
H = 128
LANES = 128
F32 = jnp.float32
BF16 = jnp.bfloat16
MESH = pl.DeviceIdType.MESH


def dft_tables():
    j = np.arange(H)[:, None]
    k = np.arange(H)[None, :]
    tables = []
    for odd in (0, 1):
        phase = 2.0 * math.pi / W * np.mod(j * (2 * k + odd), W)
        cosine = np.cos(phase) / math.sqrt(W)
        sine = np.sin(phase) / math.sqrt(W)
        tables.append(np.block([[cosine, -sine], [sine, cosine]]))
    tables += [tables[0].T, tables[1].T]
    return np.stack(tables).astype(ml_dtypes.bfloat16)


def dot(a, b):
    return jnp.dot(a, b, preferred_element_type=F32)


def neighbours(mesh_shape):
    ny, nx = mesh_shape
    y, x = lax.axis_index("gy"), lax.axis_index("gx")
    return y, x, dict(up=y > 0, down=y < ny - 1, left=x > 0, right=x < nx - 1)


def device(direction, y, x, mesh_shape):
    ny, nx = mesh_shape
    return {
        "up": (jnp.maximum(y - 1, 0), x),
        "down": (jnp.minimum(y + 1, ny - 1), x),
        "left": (y, jnp.maximum(x - 1, 0)),
        "right": (y, jnp.minimum(x + 1, nx - 1)),
    }[direction]


OPPOSITE = dict(up="down", down="up", left="right", right="left")


class Exchange:
    def __init__(self, mesh_shape, order, send, recv):
        self.shape, self.send, self.recv = mesh_shape, send, recv
        self.place = {name: axis for axis, name in enumerate(order)}
        self.order = order
        self.y, self.x, self.has = neighbours(mesh_shape)
        self.copies = []

    def target(self, direction):
        y, x = device(direction, self.y, self.x, self.shape)
        at = {"gy": y, "gx": x}
        return tuple(at[name] for name in self.order)

    def barrier(self):
        barrier = pltpu.get_barrier_semaphore()
        count = 0
        for direction, there in self.has.items():
            count = count + there.astype(jnp.int32)

            @pl.when(there)
            def _():
                pl.semaphore_signal(barrier, inc=1, device_id=self.target(direction), device_id_type=MESH)

        pl.semaphore_wait(barrier, count)

    def copy(self, direction, source, target, also=None):
        n = len(self.copies)
        descriptor = pltpu.make_async_remote_copy(
            src_ref=source, dst_ref=target, send_sem=self.send.at[n], recv_sem=self.recv.at[n],
            device_id=self.target(direction), device_id_type=MESH,
        )
        both = (lambda p: p) if also is None else (lambda p: p & self.has[also])
        self.copies.append((descriptor, both(self.has[direction]), both(self.has[OPPOSITE[direction]])))
        return n

    def start(self, n):
        descriptor, sends, _ = self.copies[n]
        pl.when(sends)(descriptor.start)

    def arrived(self, n, then=None):
        descriptor, _, receives = self.copies[n]

        @pl.when(receives)
        def _():
            descriptor.wait_recv()
            if then is not None:
                then()

    def finish(self):
        for descriptor, sends, _ in self.copies:
            pl.when(sends)(descriptor.wait_send)


def halo_kernel(mesh_shape, order, field, measured, perm, above, below, before, after, root, values, send, recv, sem):
    tile = field.shape[1]
    slots = measured.shape[0]
    loads = [
        pltpu.make_async_copy(measured.at[:, :, pl.ds(i * LANES, LANES)], values.at[:, i], sem.at[i]) for i in range(2)
    ]
    for load in loads:
        load.start()
    net = Exchange(mesh_shape, order, send, recv)
    low, mid, high = pl.ds(0, HALO), pl.ds(HALO, tile - 2 * HALO), pl.ds(tile - HALO, HALO)
    rows = {"up": (low, below), "down": (high, above)}
    vertical = {
        (direction, i): net.copy(direction, field.at[:, part, columns], target.at[:, :, columns])
        for i, columns in enumerate((low, high, mid))
        for direction, (part, target) in rows.items()
    }
    inside = pl.ds(HALO, tile)
    sides = [
        net.copy("left", field.at[:, :, low], after.at[:, inside, :]),
        net.copy("right", field.at[:, :, high], before.at[:, inside, :]),
    ]
    corners = []
    for source, also, place, direction in (
        (above, "up", pl.ds(0, HALO), "down"),
        (below, "down", pl.ds(HALO + tile, HALO), "up"),
    ):
        corners.append((direction, 0, net.copy("left", source.at[:, :, low], after.at[:, place, :], also)))
        corners.append((direction, 1, net.copy("right", source.at[:, :, high], before.at[:, place, :], also)))

    net.barrier()
    for i in (0, 1):
        for direction in rows:
            net.start(vertical[direction, i])
    for n in sides:
        net.start(n)
    for direction in rows:
        net.start(vertical[direction, 2])

    for load in loads:
        load.wait()

    @pl.loop(0, slots)
    def _(slot):
        for half in range(2):
            x = jnp.sqrt(jnp.concatenate([values[slot, i, pl.ds(half, H, stride=2), :] for i in range(2)], axis=1))
            first = x.astype(BF16)
            x = x - first.astype(F32)
            second = x.astype(BF16)
            third = (x - second.astype(F32)).astype(BF16)
            root[slot, half * H:(half + 1) * H, :] = dot(first, perm[...]) + dot(second, perm[...]) + dot(third, perm[...])

    for direction, i, n in corners:
        net.arrived(vertical[direction, i], lambda: net.start(n))
    for n in sides:
        net.arrived(n)
    for direction in rows:
        net.arrived(vertical[direction, 2])
    for _, _, n in corners:
        net.arrived(n)
    net.finish()


def halo_call(mesh_shape, order, field, measured):
    tile = field.shape[1]
    side = tile + 2 * HALO
    perm = np.zeros((W, W), np.float32)
    for k in range(W):
        perm[k, (k % 2) * H + k // 2] = 1.0
    hbm = pl.BlockSpec(memory_space=pl.ANY)
    vmem = pl.BlockSpec(memory_space=pltpu.VMEM)
    strip = jax.ShapeDtypeStruct((2, HALO, tile), F32)
    column = jax.ShapeDtypeStruct((2, side, HALO), F32)
    return pl.pallas_call(
        functools.partial(halo_kernel, mesh_shape, order),
        out_shape=(strip, strip, column, column, jax.ShapeDtypeStruct(measured.shape, F32)),
        in_specs=[hbm, hbm, vmem],
        out_specs=(hbm, hbm, hbm, hbm, vmem),
        scratch_shapes=[
            pltpu.VMEM((measured.shape[0], 2, W, LANES), F32),
            pltpu.SemaphoreType.DMA((12,)),
            pltpu.SemaphoreType.DMA((12,)),
            pltpu.SemaphoreType.DMA((2,)),
        ],
        compiler_params=pltpu.CompilerParams(collective_id=0, has_side_effects=True),
        name="halo",
    )(field, measured, jnp.asarray(perm.astype(ml_dtypes.bfloat16)))


def sum_kernel(mesh_shape, order, total, out, own, from_left, from_right, from_up, from_down, send, recv, sem):
    blocks = own.shape[1]
    side = own.shape[2]
    tile = side - 2 * HALO
    loads = [
        pltpu.make_async_copy(total.at[:, 1 + i], own.at[:, i], sem.at[i]) for i in range(blocks)
    ]
    for load in loads:
        load.start()
    net = Exchange(mesh_shape, order, send, recv)
    low, mid, high = pl.ds(0, HALO), pl.ds(HALO, tile), pl.ds(HALO + tile, HALO)
    across = {
        (direction, i): net.copy(direction, total.at[:, block, rows, :], target.at[:, rows, :])
        for i, rows in enumerate((low, high, mid))
        for direction, block, target in (("left", 0, from_right), ("right", blocks + 1, from_left))
    }
    vertical = {}
    for direction, rows, target in (("up", low, from_down), ("down", high, from_up)):
        centre = pl.ds(1, blocks - 2)
        vertical[direction, 2] = net.copy(direction, total.at[:, pl.ds(2, blocks - 2), rows, :], target.at[:, centre])
        for i, block in ((0, 0), (1, blocks - 1)):
            vertical[direction, i] = net.copy(direction, own.at[:, block, rows, :], target.at[:, block])

    net.barrier()
    for i in (0, 1):
        for direction in ("left", "right"):
            net.start(across[direction, i])
    for direction in ("up", "down"):
        net.start(vertical[direction, 2])
    for direction in ("left", "right"):
        net.start(across[direction, 2])
    for load in loads:
        load.wait()

    def add(block, rows, source):
        def then():
            own[:, block, rows, :] = own[:, block, rows, :] + source[:, rows, :]
        return then

    for i, rows, direction in ((0, low, "up"), (1, high, "down")):
        net.arrived(across["right", i], add(0, rows, from_left))
        net.start(vertical[direction, 0])
        net.arrived(across["left", i], add(blocks - 1, rows, from_right))
        net.start(vertical[direction, 1])
    net.arrived(across["right", 2], add(0, mid, from_left))
    net.arrived(across["left", 2], add(blocks - 1, mid, from_right))

    def add_rows(block, count, rows, source):
        def then():
            for i in range(block, block + count):
                own[:, i, rows, :] = own[:, i, rows, :] + source[:, i]
        return then

    first, last = pl.ds(HALO, HALO), pl.ds(tile, HALO)
    for i, block, count in ((2, 1, blocks - 2), (0, 0, 1), (1, blocks - 1, 1)):
        net.arrived(vertical["down", i], add_rows(block, count, first, from_up))
        net.arrived(vertical["up", i], add_rows(block, count, last, from_down))
    stores = [
        pltpu.make_async_copy(own.at[:, i, mid, :], out.at[:, :, pl.ds(i * LANES, LANES)], sem.at[i]) for i in range(blocks)
    ]
    for store in stores:
        store.start()
    for store in stores:
        store.wait()
    net.finish()


def sum_call(mesh_shape, order, total):
    side = total.shape[2]
    tile = side - 2 * HALO
    blocks = tile // LANES
    hbm = pl.BlockSpec(memory_space=pl.ANY)
    return pl.pallas_call(
        functools.partial(sum_kernel, mesh_shape, order),
        out_shape=jax.ShapeDtypeStruct((2, tile, tile), F32),
        in_specs=[hbm],
        out_specs=hbm,
        scratch_shapes=[
            pltpu.VMEM((2, blocks, side, LANES), F32),
            pltpu.VMEM((2, side, LANES), F32),
            pltpu.VMEM((2, side, LANES), F32),
            pltpu.VMEM((2, blocks, HALO, LANES), F32),
            pltpu.VMEM((2, blocks, HALO, LANES), F32),
            pltpu.SemaphoreType.DMA((12,)),
            pltpu.SemaphoreType.DMA((12,)),
            pltpu.SemaphoreType.DMA((blocks,)),
        ],
        compiler_params=pltpu.CompilerParams(collective_id=1, has_side_effects=True),
        name="sums",
    )(total)


def frames_kernel(
    mesh_shape, spots, count, tables, probe, root, own, above, below, before, after,
    total_out,
    ext, total, patch, stage2, wave, stage3, stage4, grad, sem,
):
    modes = probe.shape[0]
    tile = own.shape[1]
    side = tile + 2 * HALO
    blocks = tile // LANES
    _, _, has = neighbours(mesh_shape)
    n = 0
    waits = []

    def load(there, source, block, start, rows):
        nonlocal n
        copies = []
        for i in range(source.shape[2] // LANES):
            copies.append(pltpu.make_async_copy(
                source.at[:, pl.ds(start if source.shape[1] == side else 0, rows), pl.ds(i * LANES, LANES)],
                ext.at[:, block + i, pl.ds(start, rows), :], sem.at[n]))
            n += 1

        @pl.when(there)
        def _():
            for copy in copies:
                copy.start()

        @pl.when(jnp.logical_not(there))
        def _():
            for i in range(len(copies)):
                for part in range(2):
                    ext[part, block + i, start:start + rows, :] = jnp.zeros((rows, LANES), F32)

        waits.append((there, copies))

    load(jnp.asarray(True), own, 1, HALO, tile)
    load(has["up"], above, 1, 0, HALO)
    load(has["down"], below, 1, HALO + tile, HALO)
    for name, source, block in (("left", before, 0), ("right", after, 1 + blocks)):
        load(has[name], source, block, HALO, tile)
        load(has[name] & has["up"], source, block, 0, HALO)
        load(has[name] & has["down"], source, block, HALO + tile, HALO)

    @pl.loop(0, side // 16)
    def _(i):
        total[:, :, pl.ds(pl.multiple_of(i * 16, 16), 16), :] = jnp.zeros((2, total.shape[1], 16, LANES), F32)

    for there, copies in waits:
        @pl.when(there)
        def _():
            for copy in copies:
                copy.wait()

    lane = lax.broadcasted_iota(jnp.int32, (W, LANES), 1)

    @pl.loop(0, count[0, 0])
    def _(slot):
        row = spots[slot, 0]
        column = spots[slot, 1]
        block = column // LANES
        shift = column - block * LANES
        back = lax.rem(LANES - shift, LANES)
        keep = lane < LANES - shift
        for part in range(2):
            rolled = []
            for i in range(3):
                x = ext[part, block + i, pl.ds(row, W), :]
                rolled.append(pltpu.roll(x, back, axis=1))
            for i in range(2):
                patch[part, :, i * LANES:(i + 1) * LANES] = jnp.where(keep, rolled[i], rolled[i + 1])

        step = 32
        @pl.loop(0, H // step)
        def _(i):
            first = pl.multiple_of(i * step, step)
            even, odd = [], []
            for m in range(modes):
                for half in range(2):
                    rows = pl.ds(half * H + first, step)
                    pr, pi = probe[m, 0, rows, :], probe[m, 1, rows, :]
                    xr, xi = patch[0, rows, :], patch[1, rows, :]
                    re = pr * xr - pi * xi
                    im = pr * xi + pi * xr
                    even.append(jnp.concatenate([re[:, :H] + re[:, H:], im[:, :H] + im[:, H:]], axis=1))
                    odd.append(jnp.concatenate([re[:, :H] - re[:, H:], im[:, :H] - im[:, H:]], axis=1))
            even = dot(jnp.concatenate(even, axis=0).astype(BF16), tables[0])
            odd = dot(jnp.concatenate(odd, axis=0).astype(BF16), tables[1])
            for m in range(modes):
                for n, h in enumerate((even, odd)):
                    low = h[(2 * m) * step:(2 * m + 1) * step]
                    high = h[(2 * m + 1) * step:(2 * m + 2) * step]
                    plus, minus = (low + high).astype(BF16), (low - high).astype(BF16)
                    for part in range(2):
                        rows = pl.ds(part * H + first, step)
                        columns = slice(part * H, (part + 1) * H)
                        stage2[m, 0, rows, n * H:(n + 1) * H] = plus[:, columns]
                        stage2[m, 1, rows, n * H:(n + 1) * H] = minus[:, columns]

        for m in range(modes):
            for n in range(2):
                wave[m, n] = dot(tables[2 + n], stage2[m, n])

        for n in range(2):
            @pl.loop(0, H // 16)
            def _(i):
                first = pl.multiple_of(i * 16, 16)
                res = [wave[m, n, pl.ds(first, 16), :] for m in range(modes)]
                ims = [wave[m, n, pl.ds(H + first, 16), :] for m in range(modes)]
                inten = sum(x * x for x in res) + sum(x * x for x in ims)
                factor = 1.0 - root[slot, pl.ds(n * H + first, 16), :] / jnp.sqrt(inten + 1.0)
                for m in range(modes):
                    stage3[m, n, pl.ds(first, 16), :] = (factor * res[m]).astype(BF16)
                    stage3[m, n, pl.ds(H + first, 16), :] = (factor * ims[m]).astype(BF16)

        for m in range(modes):
            even = dot(tables[0], stage3[m, 0])
            odd = dot(tables[1], stage3[m, 1])
            plus, minus = (even + odd).astype(BF16), (even - odd).astype(BF16)
            for half, x in enumerate((plus, minus)):
                for part in range(2):
                    for n in range(2):
                        stage4[n, m, half * H:(half + 1) * H, part * H:(part + 1) * H] = x[part * H:(part + 1) * H, n * H:(n + 1) * H]

        @pl.loop(0, W // step)
        def _(i):
            rows = pl.ds(pl.multiple_of(i * step, step), step)
            even = dot(stage4[0, :, rows, :].reshape(modes * step, W), tables[2])
            odd = dot(stage4[1, :, rows, :].reshape(modes * step, W), tables[3])
            plus, minus = even + odd, even - odd
            for half, x in enumerate((plus, minus)):
                columns = slice(half * H, (half + 1) * H)
                gr = gi = 0.0
                for m in range(modes):
                    pr, pi = probe[m, 0, rows, columns], probe[m, 1, rows, columns]
                    cr, ci = x[m * step:(m + 1) * step, :H], x[m * step:(m + 1) * step, H:]
                    gr = gr + (pr * cr + pi * ci)
                    gi = gi + (pr * ci - pi * cr)
                grad[0, rows, columns] = gr
                grad[1, rows, columns] = gi

        moved = lane >= shift
        for part in range(2):
            left = pltpu.roll(grad[part, :, 0:LANES], shift, axis=1)
            right = pltpu.roll(grad[part, :, LANES:2 * LANES], shift, axis=1)
            zero = jnp.zeros_like(left)
            pieces = (jnp.where(moved, left, zero), jnp.where(moved, right, left), jnp.where(moved, zero, right))
            for i, piece in enumerate(pieces):
                where = (part, block + i, pl.ds(row, W), slice(None))
                total[where] = total[where] + piece

    copies = [
        pltpu.make_async_copy(total.at[:, i], total_out.at[:, i], sem.at[i])
        for i in range(side // LANES)
    ]
    for copy in copies:
        copy.start()
    for copy in copies:
        copy.wait()


def frames_call(mesh_shape, spots, count, probe, root, own, above, below, before, after):
    modes = probe.shape[0]
    side = own.shape[1] + 2 * HALO
    wide = side + LANES
    smem = pl.BlockSpec(memory_space=pltpu.SMEM)
    vmem = pl.BlockSpec(memory_space=pltpu.VMEM)
    hbm = pl.BlockSpec(memory_space=pl.ANY)
    return pl.pallas_call(
        functools.partial(frames_kernel, mesh_shape),
        out_shape=jax.ShapeDtypeStruct((2, side // LANES, side, LANES), F32),
        in_specs=[smem, smem, vmem, vmem, vmem, hbm, hbm, hbm, hbm, hbm],
        out_specs=hbm,
        scratch_shapes=[
            pltpu.VMEM((2, wide // LANES, side, LANES), F32),
            pltpu.VMEM((2, wide // LANES, side, LANES), F32),
            pltpu.VMEM((2, W, W), F32),
            pltpu.VMEM((modes, 2, W, W), BF16),
            pltpu.VMEM((modes, 2, W, W), F32),
            pltpu.VMEM((modes, 2, W, W), BF16),
            pltpu.VMEM((2, modes, W, W), BF16),
            pltpu.VMEM((2, W, W), F32),
            pltpu.SemaphoreType.DMA((32,)),
        ],
        compiler_params=pltpu.CompilerParams(vmem_limit_bytes=60 * 1024 * 1024),
        name="frames",
    )(spots, count, jnp.asarray(dft_tables()), probe, root, own, above, below, before, after)


def body(mesh_shape, order, object_field, probe, positions, frame_count, measured):
    above, below, before, after, root = halo_call(mesh_shape, order, object_field, measured[0, 0])
    total = frames_call(mesh_shape, positions[0, 0], frame_count, probe, root, object_field, above, below, before, after)
    return sum_call(mesh_shape, order, total)


def solution(mesh):
    mesh_shape = (mesh.shape["gy"], mesh.shape["gx"])
    return jax.shard_map(
        functools.partial(body, mesh_shape, tuple(mesh.axis_names)),
        mesh=mesh,
        in_specs=(
            P(None, "gy", "gx"),
            P(),
            P("gy", "gx", None, None),
            P("gy", "gx"),
            P("gy", "gx", None, None, None),
        ),
        out_specs=P(None, "gy", "gx"),
        check_vma=False,
    )
```

```python
import functools
import math

import jax
import jax.numpy as jnp
import ml_dtypes
import numpy as np
from jax import lax
from jax.experimental import pallas as pl
from jax.experimental.pallas import tpu as pltpu
from jax.sharding import PartitionSpec as P

HALO = 128
W = 256
H = 128
LANES = 128
F32 = jnp.float32
BF16 = jnp.bfloat16
MESH = pl.DeviceIdType.MESH


def dft_tables():
    j = np.arange(H)[:, None]
    k = np.arange(H)[None, :]
    tables = []
    for odd in (0, 1):
        phase = 2.0 * math.pi / W * np.mod(j * (2 * k + odd), W)
        cosine = np.cos(phase) / math.sqrt(W)
        sine = np.sin(phase) / math.sqrt(W)
        tables.append(np.block([[cosine, -sine], [sine, cosine]]))
    tables += [tables[0].T, tables[1].T]
    return np.stack(tables).astype(ml_dtypes.bfloat16)


def dot(a, b):
    return jnp.dot(a, b, preferred_element_type=F32)


def neighbours(mesh_shape):
    ny, nx = mesh_shape
    y, x = lax.axis_index("gy"), lax.axis_index("gx")
    return y, x, dict(up=y > 0, down=y < ny - 1, left=x > 0, right=x < nx - 1)


def device(direction, y, x, mesh_shape):
    ny, nx = mesh_shape
    return {
        "up": (jnp.maximum(y - 1, 0), x),
        "down": (jnp.minimum(y + 1, ny - 1), x),
        "left": (y, jnp.maximum(x - 1, 0)),
        "right": (y, jnp.minimum(x + 1, nx - 1)),
    }[direction]


OPPOSITE = dict(up="down", down="up", left="right", right="left")


class Exchange:
    def __init__(self, mesh_shape, order, send, recv):
        self.shape, self.send, self.recv = mesh_shape, send, recv
        self.place = {name: axis for axis, name in enumerate(order)}
        self.order = order
        self.y, self.x, self.has = neighbours(mesh_shape)
        self.copies = []

    def target(self, direction):
        y, x = device(direction, self.y, self.x, self.shape)
        at = {"gy": y, "gx": x}
        return tuple(at[name] for name in self.order)

    def barrier(self):
        barrier = pltpu.get_barrier_semaphore()
        count = 0
        for direction, there in self.has.items():
            count = count + there.astype(jnp.int32)

            @pl.when(there)
            def _():
                pl.semaphore_signal(barrier, inc=1, device_id=self.target(direction), device_id_type=MESH)

        pl.semaphore_wait(barrier, count)

    def copy(self, direction, source, target, also=None):
        n = len(self.copies)
        descriptor = pltpu.make_async_remote_copy(
            src_ref=source, dst_ref=target, send_sem=self.send.at[n], recv_sem=self.recv.at[n],
            device_id=self.target(direction), device_id_type=MESH,
        )
        both = (lambda p: p) if also is None else (lambda p: p & self.has[also])
        self.copies.append((descriptor, both(self.has[direction]), both(self.has[OPPOSITE[direction]])))
        return n

    def start(self, n):
        descriptor, sends, _ = self.copies[n]
        pl.when(sends)(descriptor.start)

    def arrived(self, n, then=None):
        descriptor, _, receives = self.copies[n]

        @pl.when(receives)
        def _():
            descriptor.wait_recv()
            if then is not None:
                then()

    def finish(self):
        for descriptor, sends, _ in self.copies:
            pl.when(sends)(descriptor.wait_send)


def halo_kernel(mesh_shape, order, field, measured, perm, ext, root, values, send, recv, sem):
    tile = field.shape[1]
    slots = measured.shape[0]
    blocks = tile // LANES
    loads = [
        pltpu.make_async_copy(measured.at[:, :, pl.ds(i * LANES, LANES)], values.at[:, i], sem.at[i]) for i in range(2)
    ]
    net = Exchange(mesh_shape, order, send, recv)
    inside = pl.ds(HALO, tile)
    rows = {"up": (pl.ds(0, HALO), pl.ds(HALO + tile, HALO)), "down": (pl.ds(tile - HALO, HALO), pl.ds(0, HALO))}
    column = [pl.ds(i * LANES, LANES) for i in range(blocks)]
    inner = range(1, blocks - 1)
    vertical = {
        (direction, i): net.copy(direction, field.at[:, part, column[i]], ext.at[:, 1 + i, place, :])
        for i in (0, blocks - 1, *inner)
        for direction, (part, place) in rows.items()
    }
    sides = [
        net.copy("left", field.at[:, :, column[0]], ext.at[:, 1 + blocks, inside, :]),
        net.copy("right", field.at[:, :, column[-1]], ext.at[:, 0, inside, :]),
    ]
    corners = []
    for direction, also in (("down", "up"), ("up", "down")):
        place = rows[direction][1]
        for i, block, towards, target in ((0, 1, "left", 1 + blocks), (blocks - 1, blocks, "right", 0)):
            n = net.copy(towards, ext.at[:, block, place, :], ext.at[:, target, place, :], also)
            corners.append((direction, i, n))

    net.barrier()
    for i in (0, blocks - 1):
        for direction in rows:
            net.start(vertical[direction, i])
    for n in sides:
        net.start(n)
    for i in inner:
        for direction in rows:
            net.start(vertical[direction, i])
    own = [pltpu.make_async_copy(field.at[:, :, column[i]], ext.at[:, 1 + i, inside, :], sem.at[2 + i]) for i in range(blocks)]
    for load in loads + own:
        load.start()

    def clear(there, blocks, first, count):
        @pl.when(jnp.logical_not(there))
        def _():
            for block in blocks:
                for part in range(2):
                    ext[part, block, first:first + count, :] = jnp.zeros((count, LANES), F32)

    has = net.has
    middle = range(1, 1 + blocks)
    clear(has["up"], middle, 0, HALO)
    clear(has["down"], middle, HALO + tile, HALO)
    for direction, block in (("left", 0), ("right", 1 + blocks)):
        clear(has[direction], (block,), HALO, tile)
        clear(has[direction] & has["up"], (block,), 0, HALO)
        clear(has[direction] & has["down"], (block,), HALO + tile, HALO)
    for load in loads:
        load.wait()

    @pl.loop(0, slots)
    def _(slot):
        for half in range(2):
            x = jnp.sqrt(jnp.concatenate([values[slot, i, pl.ds(half, H, stride=2), :] for i in range(2)], axis=1))
            first = x.astype(BF16)
            x = x - first.astype(F32)
            second = x.astype(BF16)
            third = (x - second.astype(F32)).astype(BF16)
            root[slot, half * H:(half + 1) * H, :] = dot(first, perm[...]) + dot(second, perm[...]) + dot(third, perm[...])

    for load in own:
        load.wait()
    for direction, i, n in corners:
        net.arrived(vertical[direction, i], lambda: net.start(n))
    for n in sides:
        net.arrived(n)
    for i in inner:
        for direction in rows:
            net.arrived(vertical[direction, i])
    for _, _, n in corners:
        net.arrived(n)
    net.finish()


def halo_call(mesh_shape, order, field, measured):
    tile = field.shape[1]
    side = tile + 2 * HALO
    perm = np.zeros((W, W), np.float32)
    for k in range(W):
        perm[k, (k % 2) * H + k // 2] = 1.0
    hbm = pl.BlockSpec(memory_space=pltpu.HBM)
    vmem = pl.BlockSpec(memory_space=pltpu.VMEM)
    blocks = tile // LANES
    n = 2 * blocks + 6
    return pl.pallas_call(
        functools.partial(halo_kernel, mesh_shape, order),
        out_shape=(
            jax.ShapeDtypeStruct((2, blocks + 3, side, LANES), F32),
            jax.ShapeDtypeStruct(measured.shape, F32),
        ),
        in_specs=[hbm, hbm, vmem],
        out_specs=(vmem, vmem),
        scratch_shapes=[
            pltpu.VMEM((measured.shape[0], 2, W, LANES), F32),
            pltpu.SemaphoreType.DMA((n,)),
            pltpu.SemaphoreType.DMA((n,)),
            pltpu.SemaphoreType.DMA((2 + blocks,)),
        ],
        compiler_params=pltpu.CompilerParams(collective_id=0, has_side_effects=True, vmem_limit_bytes=12 * 1024 * 1024),
        name="halo",
    )(field, measured, jnp.asarray(perm.astype(ml_dtypes.bfloat16)))


def sum_kernel(mesh_shape, order, total, out, edges, from_left, from_right, from_up, from_down, send, recv):
    side = total.shape[2]
    tile = side - 2 * HALO
    blocks = tile // LANES
    net = Exchange(mesh_shape, order, send, recv)
    low, mid, high = pl.ds(0, HALO), pl.ds(HALO, tile), pl.ds(HALO + tile, HALO)
    across = {
        (direction, i): net.copy(direction, total.at[:, block, rows, :], target.at[:, rows, :])
        for i, rows in enumerate((low, high, mid))
        for direction, block, target in (("left", 0, from_right), ("right", blocks + 1, from_left))
    }
    vertical = {}
    for k, (direction, rows, target) in enumerate((("up", low, from_down), ("down", high, from_up))):
        centre = pl.ds(1, blocks - 2)
        vertical[direction, 2] = net.copy(direction, total.at[:, pl.ds(2, blocks - 2), rows, :], target.at[:, centre])
        for i, block in ((0, 0), (1, blocks - 1)):
            vertical[direction, i] = net.copy(direction, edges.at[k, i], target.at[:, block])

    net.barrier()
    for i in (0, 1):
        for direction in ("left", "right"):
            net.start(across[direction, i])
    for direction in ("up", "down"):
        net.start(vertical[direction, 2])
    for direction in ("left", "right"):
        net.start(across[direction, 2])

    for i in range(blocks):
        out[:, :, i * LANES:(i + 1) * LANES] = total[:, 1 + i, HALO:HALO + tile, :]
    for k, rows in enumerate((low, high)):
        for i, block in ((0, 1), (1, blocks)):
            edges[k, i] = total[:, block, rows, :]

    for k, (rows, direction) in enumerate(((low, "up"), (high, "down"))):
        for i, towards, source in ((0, "right", from_left), (1, "left", from_right)):
            def add():
                edges[k, i] = edges[k, i] + source[:, rows, :]

            net.arrived(across[towards, k], add)
            net.start(vertical[direction, i])

    for i, towards, source in ((0, "right", from_left), (blocks - 1, "left", from_right)):
        def add():
            columns = slice(i * LANES, (i + 1) * LANES)
            out[:, :, columns] = out[:, :, columns] + source[:, mid, :]

        net.arrived(across[towards, 2], add)

    for i, parts in ((2, range(1, blocks - 1)), (0, (0,)), (1, (blocks - 1,))):
        for towards, first, source in (("down", 0, from_up), ("up", tile - HALO, from_down)):
            def add():
                for part in parts:
                    place = (slice(None), slice(first, first + HALO), slice(part * LANES, (part + 1) * LANES))
                    out[place] = out[place] + source[:, part]

            net.arrived(vertical[towards, i], add)
    net.finish()


def sum_call(mesh_shape, order, total):
    side = total.shape[2]
    tile = side - 2 * HALO
    blocks = tile // LANES
    vmem = pl.BlockSpec(memory_space=pltpu.VMEM)
    return pl.pallas_call(
        functools.partial(sum_kernel, mesh_shape, order),
        out_shape=jax.ShapeDtypeStruct((2, tile, tile), F32),
        in_specs=[vmem],
        out_specs=vmem,
        scratch_shapes=[
            pltpu.VMEM((2, 2, 2, HALO, LANES), F32),
            pltpu.VMEM((2, side, LANES), F32),
            pltpu.VMEM((2, side, LANES), F32),
            pltpu.VMEM((2, blocks, HALO, LANES), F32),
            pltpu.VMEM((2, blocks, HALO, LANES), F32),
            pltpu.SemaphoreType.DMA((12,)),
            pltpu.SemaphoreType.DMA((12,)),
        ],
        compiler_params=pltpu.CompilerParams(collective_id=1, has_side_effects=True, vmem_limit_bytes=16 * 1024 * 1024),
        name="sums",
    )(total)


def frames_kernel(
    spots, count, tables, probe, root, ext,
    total,
    patch, stage2, wave, stage3, stage4, grad,
):
    modes = probe.shape[0]

    @pl.loop(0, total.shape[2] // 16)
    def _(i):
        total[:, :, pl.ds(pl.multiple_of(i * 16, 16), 16), :] = jnp.zeros((2, total.shape[1], 16, LANES), F32)

    lane = lax.broadcasted_iota(jnp.int32, (W, LANES), 1)

    @pl.loop(0, count[0, 0])
    def _(slot):
        row = spots[0, 0, 0, slot]
        column = spots[0, 0, 1, slot]
        block = column // LANES
        shift = column - block * LANES
        back = lax.rem(LANES - shift, LANES)
        keep = lane < LANES - shift
        for part in range(2):
            rolled = []
            for i in range(3):
                x = ext[part, block + i, pl.ds(row, W), :]
                rolled.append(pltpu.roll(x, back, axis=1))
            for i in range(2):
                patch[part, :, i * LANES:(i + 1) * LANES] = jnp.where(keep, rolled[i], rolled[i + 1])

        step = 64
        for first in range(0, H, step):
            even, odd = [], []
            for m in range(modes):
                for half in range(2):
                    rows = pl.ds(half * H + first, step)
                    pr, pi = probe[m, 0, rows, :], probe[m, 1, rows, :]
                    xr, xi = patch[0, rows, :], patch[1, rows, :]
                    re = pr * xr - pi * xi
                    im = pr * xi + pi * xr
                    even.append(jnp.concatenate([re[:, :H] + re[:, H:], im[:, :H] + im[:, H:]], axis=1))
                    odd.append(jnp.concatenate([re[:, :H] - re[:, H:], im[:, :H] - im[:, H:]], axis=1))
            even = dot(jnp.concatenate(even, axis=0).astype(BF16), tables[0])
            odd = dot(jnp.concatenate(odd, axis=0).astype(BF16), tables[1])
            for m in range(modes):
                for n, h in enumerate((even, odd)):
                    low = h[(2 * m) * step:(2 * m + 1) * step]
                    high = h[(2 * m + 1) * step:(2 * m + 2) * step]
                    plus, minus = (low + high).astype(BF16), (low - high).astype(BF16)
                    for part in range(2):
                        rows = pl.ds(part * H + first, step)
                        columns = slice(part * H, (part + 1) * H)
                        stage2[m, 0, rows, n * H:(n + 1) * H] = plus[:, columns]
                        stage2[m, 1, rows, n * H:(n + 1) * H] = minus[:, columns]

        for n in range(2):
            for m in range(modes):
                wave[m, n] = dot(tables[2 + n], stage2[m, n])
            for first in range(0, H, 16):
                res = [wave[m, n, pl.ds(first, 16), :] for m in range(modes)]
                ims = [wave[m, n, pl.ds(H + first, 16), :] for m in range(modes)]
                inten = sum(x * x for x in res[1:] + ims) + res[0] * res[0]
                factor = 1.0 - root[slot, pl.ds(n * H + first, 16), :] / jnp.sqrt(inten + 1.0)
                for m in range(modes):
                    stage3[m, n, pl.ds(first, 16), :] = (factor * res[m]).astype(BF16)
                    stage3[m, n, pl.ds(H + first, 16), :] = (factor * ims[m]).astype(BF16)

        for m in range(modes):
            even = dot(tables[0], stage3[m, 0])
            odd = dot(tables[1], stage3[m, 1])
            plus, minus = (even + odd).astype(BF16), (even - odd).astype(BF16)
            for half, x in enumerate((plus, minus)):
                for part in range(2):
                    for n in range(2):
                        stage4[n, m, half * H:(half + 1) * H, part * H:(part + 1) * H] = x[part * H:(part + 1) * H, n * H:(n + 1) * H]

        step = 64
        for first in range(0, W, step):
            rows = pl.ds(first, step)
            even = dot(stage4[0, :, rows, :].reshape(modes * step, W), tables[2])
            odd = dot(stage4[1, :, rows, :].reshape(modes * step, W), tables[3])
            plus, minus = even + odd, even - odd
            for half, x in enumerate((plus, minus)):
                columns = slice(half * H, (half + 1) * H)
                gr = gi = None
                for m in range(modes):
                    pr, pi = probe[m, 0, rows, columns], probe[m, 1, rows, columns]
                    cr, ci = x[m * step:(m + 1) * step, :H], x[m * step:(m + 1) * step, H:]
                    re, im = pr * cr + pi * ci, pr * ci - pi * cr
                    gr, gi = (re, im) if gr is None else (gr + re, gi + im)
                grad[0, rows, columns] = gr
                grad[1, rows, columns] = gi

        moved = lane >= shift
        for part in range(2):
            left = pltpu.roll(grad[part, :, 0:LANES], shift, axis=1)
            right = pltpu.roll(grad[part, :, LANES:2 * LANES], shift, axis=1)
            zero = jnp.zeros_like(left)
            pieces = (jnp.where(moved, left, zero), jnp.where(moved, right, left), jnp.where(moved, zero, right))
            for i, piece in enumerate(pieces):
                where = (part, block + i, pl.ds(row, W), slice(None))
                total[where] = total[where] + piece


def frames_call(spots, count, probe, root, ext):
    modes = probe.shape[0]
    smem = pl.BlockSpec(memory_space=pltpu.SMEM)
    vmem = pl.BlockSpec(memory_space=pltpu.VMEM)
    return pl.pallas_call(
        frames_kernel,
        out_shape=jax.ShapeDtypeStruct(ext.shape, F32),
        in_specs=[smem, smem, vmem, vmem, vmem, vmem],
        out_specs=vmem,
        scratch_shapes=[
            pltpu.VMEM((2, W, W), F32),
            pltpu.VMEM((modes, 2, W, W), BF16),
            pltpu.VMEM((modes, 2, W, W), F32),
            pltpu.VMEM((modes, 2, W, W), BF16),
            pltpu.VMEM((2, modes, W, W), BF16),
            pltpu.VMEM((2, W, W), F32),
        ],
        compiler_params=pltpu.CompilerParams(vmem_limit_bytes=28 * 1024 * 1024),
        name="frames",
    )(spots, count, jnp.asarray(dft_tables()), probe, root, ext)


def body(mesh_shape, order, object_field, probe, positions, frame_count, measured):
    ext, root = halo_call(mesh_shape, order, object_field, measured[0, 0])
    total = frames_call(jnp.swapaxes(positions, 2, 3), frame_count, probe, root, ext)
    return sum_call(mesh_shape, order, total)


def solution(mesh):
    mesh_shape = (mesh.shape["gy"], mesh.shape["gx"])
    return jax.shard_map(
        functools.partial(body, mesh_shape, tuple(mesh.axis_names)),
        mesh=mesh,
        in_specs=(
            P(None, "gy", "gx"),
            P(),
            P("gy", "gx", None, None),
            P("gy", "gx"),
            P("gy", "gx", None, None, None),
        ),
        out_specs=P(None, "gy", "gx"),
        check_vma=False,
    )
```

```python
import functools
import math

import jax
import jax.numpy as jnp
import ml_dtypes
import numpy as np
from jax import lax
from jax.experimental import pallas as pl
from jax.experimental.pallas import tpu as pltpu
from jax.sharding import PartitionSpec as P

HALO = 128
W = 256
H = 128
LANES = 128
F32 = jnp.float32
BF16 = jnp.bfloat16
MESH = pl.DeviceIdType.MESH


def dft_tables():
    j = np.arange(H)[:, None]
    k = np.arange(H)[None, :]
    tables = []
    for odd in (0, 1):
        phase = 2.0 * math.pi / W * np.mod(j * (2 * k + odd), W)
        cosine = np.cos(phase) / math.sqrt(W)
        sine = np.sin(phase) / math.sqrt(W)
        tables.append(np.block([[cosine, -sine], [sine, cosine]]))
    tables += [tables[0].T, tables[1].T]
    return np.stack(tables).astype(ml_dtypes.bfloat16)


def dot(a, b):
    return jnp.dot(a, b, preferred_element_type=F32)


def neighbours(mesh_shape):
    ny, nx = mesh_shape
    y, x = lax.axis_index("gy"), lax.axis_index("gx")
    return y, x, dict(up=y > 0, down=y < ny - 1, left=x > 0, right=x < nx - 1)


def device(direction, y, x, mesh_shape):
    ny, nx = mesh_shape
    return {
        "up": (jnp.maximum(y - 1, 0), x),
        "down": (jnp.minimum(y + 1, ny - 1), x),
        "left": (y, jnp.maximum(x - 1, 0)),
        "right": (y, jnp.minimum(x + 1, nx - 1)),
    }[direction]


RELAYS = (("above", "last"), ("last", "below"), ("below", "first"), ("first", "above"))
NEXT = dict(above="below", below="above")
OPPOSITE = dict(up="down", down="up", left="right", right="left")


class Exchange:
    def __init__(self, mesh_shape, order, send, recv):
        self.shape, self.send, self.recv = mesh_shape, send, recv
        self.order = order
        self.y, self.x, self.has = neighbours(mesh_shape)
        ny = mesh_shape[0]
        self.rows = {"first": 0, "above": ny // 2 - 1, "below": ny // 2, "last": ny - 1}
        self.copies = []

    def at(self, y, x):
        at = {"gy": y, "gx": x}
        return tuple(at[name] for name in self.order)

    def target(self, direction):
        return self.at(*device(direction, self.y, self.x, self.shape))

    def barrier(self):
        barrier = pltpu.get_barrier_semaphore()
        count = 0
        meets = [(there, self.target(direction)) for direction, there in self.has.items()]
        for a, b in RELAYS:
            for y, other in ((self.rows[a], self.rows[b]), (self.rows[b], self.rows[a])):
                meets.append((self.y == y, self.at(other, self.x)))
        for there, device in meets:
            count = count + there.astype(jnp.int32)

            @pl.when(there)
            def _():
                pl.semaphore_signal(barrier, inc=1, device_id=device, device_id_type=MESH)

        pl.semaphore_wait(barrier, count)

    def add(self, source, target, device, sends, receives):
        n = len(self.copies)
        descriptor = pltpu.make_async_remote_copy(
            src_ref=source, dst_ref=target, send_sem=self.send.at[n], recv_sem=self.recv.at[n],
            device_id=device, device_id_type=MESH,
        )
        self.copies.append((descriptor, sends, receives))
        return n

    def copy(self, direction, source, target, also=None, but=None):
        sends, receives = self.has[direction], self.has[OPPOSITE[direction]]
        if also is not None:
            sends, receives = sends & self.has[also], receives & self.has[also]
        if but is not None:
            sends, receives = sends & (self.y != self.rows[but]), receives & (self.y != self.rows[NEXT[but]])
        return self.add(source, target, self.target(direction), sends, receives)

    def relayed(self, a, b, c, source, buffer, target):
        first, by, last = self.rows[a], self.rows[b], self.rows[c]
        return (
            self.add(source, buffer, self.at(by, self.x), self.y == first, self.y == by),
            self.add(buffer, target, self.at(last, self.x), self.y == by, self.y == last),
        )

    def start(self, n):
        descriptor, sends, _ = self.copies[n]
        pl.when(sends)(descriptor.start)

    def arrived(self, n, then=None):
        descriptor, _, receives = self.copies[n]

        @pl.when(receives)
        def _():
            descriptor.wait_recv()
            if then is not None:
                then()

    def finish(self):
        for descriptor, sends, _ in self.copies:
            pl.when(sends)(descriptor.wait_send)


def halo_kernel(mesh_shape, order, field, measured, ext, root, values, perm, relay, send, recv, sem):
    tile = field.shape[1]
    slots = measured.shape[0]
    blocks = tile // LANES
    loads = [
        pltpu.make_async_copy(measured.at[:, :, pl.ds(i * LANES, LANES)], values.at[:, i], sem.at[i]) for i in range(2)
    ]
    net = Exchange(mesh_shape, order, send, recv)
    inside = pl.ds(HALO, tile)
    rows = {"up": (pl.ds(0, HALO), pl.ds(HALO + tile, HALO)), "down": (pl.ds(tile - HALO, HALO), pl.ds(0, HALO))}
    column = [pl.ds(i * LANES, LANES) for i in range(blocks)]
    inner = range(1, blocks - 1)
    crossing = {"down": ("above", "last", "below"), "up": ("below", "first", "above")}
    vertical, around = {}, []
    for i in (0, blocks - 1, *inner):
        for direction, (part, place) in rows.items():
            source, target = field.at[:, part, column[i]], ext.at[:, 1 + i, place, :]
            but = crossing[direction][0] if i in inner else None
            vertical[direction, i] = net.copy(direction, source, target, but=but)
            if i in inner:
                around.append(net.relayed(*crossing[direction], source, relay.at[:, len(around)], target))
    sides = [
        net.copy("left", field.at[:, :, column[0]], ext.at[:, 1 + blocks, inside, :]),
        net.copy("right", field.at[:, :, column[-1]], ext.at[:, 0, inside, :]),
    ]
    corners = []
    for direction, also in (("down", "up"), ("up", "down")):
        place = rows[direction][1]
        for i, block, towards, target in ((0, 1, "left", 1 + blocks), (blocks - 1, blocks, "right", 0)):
            n = net.copy(towards, ext.at[:, block, place, :], ext.at[:, target, place, :], also)
            corners.append((direction, i, n))

    net.barrier()
    for first, _ in around:
        net.start(first)
    for i in (0, blocks - 1):
        for direction in rows:
            net.start(vertical[direction, i])
    for n in sides:
        net.start(n)
    for i in inner:
        for direction in rows:
            net.start(vertical[direction, i])
    own = [pltpu.make_async_copy(field.at[:, :, column[i]], ext.at[:, 1 + i, inside, :], sem.at[2 + i]) for i in range(blocks)]
    for load in loads + own:
        load.start()

    def clear(there, blocks, first, count):
        @pl.when(jnp.logical_not(there))
        def _():
            for block in blocks:
                for part in range(2):
                    ext[part, block, first:first + count, :] = jnp.zeros((count, LANES), F32)

    has = net.has
    middle = range(1, 1 + blocks)
    clear(has["up"], middle, 0, HALO)
    clear(has["down"], middle, HALO + tile, HALO)
    for direction, block in (("left", 0), ("right", 1 + blocks)):
        clear(has[direction], (block,), HALO, tile)
        clear(has[direction] & has["up"], (block,), 0, HALO)
        clear(has[direction] & has["down"], (block,), HALO + tile, HALO)
    k = lax.broadcasted_iota(jnp.int32, (W, W), 0)
    perm[...] = (lax.broadcasted_iota(jnp.int32, (W, W), 1) == (k % 2) * H + k // 2).astype(F32).astype(BF16)
    for load in loads:
        load.wait()

    @pl.loop(0, slots)
    def _(slot):
        for half in range(2):
            x = jnp.sqrt(jnp.concatenate([values[slot, i, pl.ds(half, H, stride=2), :] for i in range(2)], axis=1))
            first = x.astype(BF16)
            x = x - first.astype(F32)
            second = x.astype(BF16)
            third = (x - second.astype(F32)).astype(BF16)
            root[slot, half * H:(half + 1) * H, :] = dot(first, perm[...]) + dot(second, perm[...]) + dot(third, perm[...])

    for load in own:
        load.wait()
    for direction, i, n in corners:
        net.arrived(vertical[direction, i], lambda: net.start(n))
    for first, second in around:
        net.arrived(first, lambda: net.start(second))
    for n in sides:
        net.arrived(n)
    for _, second in around:
        net.arrived(second)
    for i in inner:
        for direction in rows:
            net.arrived(vertical[direction, i])
    for _, _, n in corners:
        net.arrived(n)
    net.finish()


def halo_call(mesh_shape, order, field, measured):
    tile = field.shape[1]
    side = tile + 2 * HALO
    hbm = pl.BlockSpec(memory_space=pltpu.HBM)
    vmem = pl.BlockSpec(memory_space=pltpu.VMEM)
    blocks = tile // LANES
    inner = blocks - 2
    n = 2 * blocks + 6 + 4 * inner
    return pl.pallas_call(
        functools.partial(halo_kernel, mesh_shape, order),
        out_shape=(
            jax.ShapeDtypeStruct((2, blocks + 3, side, LANES), F32),
            jax.ShapeDtypeStruct(measured.shape, F32),
        ),
        in_specs=[hbm, hbm],
        out_specs=(vmem, vmem),
        scratch_shapes=[
            pltpu.VMEM((measured.shape[0], 2, W, LANES), F32),
            pltpu.VMEM((W, W), BF16),
            pltpu.VMEM((2, 2 * inner, HALO, LANES), F32),
            pltpu.SemaphoreType.DMA((n,)),
            pltpu.SemaphoreType.DMA((n,)),
            pltpu.SemaphoreType.DMA((2 + blocks,)),
        ],
        compiler_params=pltpu.CompilerParams(collective_id=0, has_side_effects=True, vmem_limit_bytes=12 * 1024 * 1024),
        name="halo",
    )(pltpu.with_memory_space_constraint(field, pltpu.HBM), pltpu.with_memory_space_constraint(measured, pltpu.HBM))


def sum_kernel(mesh_shape, order, total, out, edges, from_left, from_right, from_up, from_down, send, recv):
    side = total.shape[2]
    tile = side - 2 * HALO
    blocks = tile // LANES
    net = Exchange(mesh_shape, order, send, recv)
    low, mid, high = pl.ds(0, HALO), pl.ds(HALO, tile), pl.ds(HALO + tile, HALO)
    across = {
        (direction, i): net.copy(direction, total.at[:, block, rows, :], target.at[:, rows, :])
        for i, rows in enumerate((low, high, mid))
        for direction, block, target in (("left", 0, from_right), ("right", blocks + 1, from_left))
    }
    crossing = {"down": ("above", "last", "below"), "up": ("below", "first", "above")}
    vertical, around = {}, {}
    for k, (direction, rows, target, relay) in enumerate((("up", low, from_down, from_up), ("down", high, from_up, from_down))):
        for i in range(1, blocks - 1):
            source, place = total.at[:, 1 + i, rows, :], target.at[:, i]
            vertical[direction, 1 + i] = net.copy(direction, source, place, but=crossing[direction][0])
            around[direction, 1 + i] = net.relayed(*crossing[direction], source, relay.at[:, i], place)
        for i, block in ((0, 0), (1, blocks - 1)):
            vertical[direction, i] = net.copy(direction, edges.at[k, i], target.at[:, block])

    net.barrier()
    for i in (0, 1):
        for direction in ("left", "right"):
            net.start(across[direction, i])
    for first, _ in around.values():
        net.start(first)
    for i in range(1, blocks - 1):
        for direction in ("up", "down"):
            net.start(vertical[direction, 1 + i])
    for direction in ("left", "right"):
        net.start(across[direction, 2])

    for i in range(blocks):
        out[:, :, i * LANES:(i + 1) * LANES] = total[:, 1 + i, HALO:HALO + tile, :]
    for k, rows in enumerate((low, high)):
        for i, block in ((0, 1), (1, blocks)):
            edges[k, i] = total[:, block, rows, :]

    for k, (rows, direction) in enumerate(((low, "up"), (high, "down"))):
        for i, towards, source in ((0, "right", from_left), (1, "left", from_right)):
            def add():
                edges[k, i] = edges[k, i] + source[:, rows, :]

            net.arrived(across[towards, k], add)
            net.start(vertical[direction, i])

    for first, second in around.values():
        net.arrived(first, lambda: net.start(second))

    for i, towards, source in ((0, "right", from_left), (blocks - 1, "left", from_right)):
        def add():
            columns = slice(i * LANES, (i + 1) * LANES)
            out[:, :, columns] = out[:, :, columns] + source[:, mid, :]

        net.arrived(across[towards, 2], add)

    for i, part in (*((1 + part, part) for part in range(1, blocks - 1)), (0, 0), (1, blocks - 1)):
        for towards, first, source in (("down", 0, from_up), ("up", tile - HALO, from_down)):
            def add():
                place = (slice(None), slice(first, first + HALO), slice(part * LANES, (part + 1) * LANES))
                out[place] = out[place] + source[:, part]

            net.arrived(vertical[towards, i], add)
            if i > 1:
                net.arrived(around[towards, i][1], add)
    net.finish()


def sum_call(mesh_shape, order, total):
    side = total.shape[2]
    tile = side - 2 * HALO
    blocks = tile // LANES
    n = 6 + 2 * blocks + 4 * (blocks - 2)
    vmem = pl.BlockSpec(memory_space=pltpu.VMEM)
    return pl.pallas_call(
        functools.partial(sum_kernel, mesh_shape, order),
        out_shape=jax.ShapeDtypeStruct((2, tile, tile), F32),
        in_specs=[vmem],
        out_specs=vmem,
        scratch_shapes=[
            pltpu.VMEM((2, 2, 2, HALO, LANES), F32),
            pltpu.VMEM((2, side, LANES), F32),
            pltpu.VMEM((2, side, LANES), F32),
            pltpu.VMEM((2, blocks, HALO, LANES), F32),
            pltpu.VMEM((2, blocks, HALO, LANES), F32),
            pltpu.SemaphoreType.DMA((n,)),
            pltpu.SemaphoreType.DMA((n,)),
        ],
        compiler_params=pltpu.CompilerParams(collective_id=1, has_side_effects=True, vmem_limit_bytes=16 * 1024 * 1024),
        name="sums",
    )(total)


def frames_kernel(
    spots, count, tables, probe, root, ext,
    total,
    patch, stage2, wave, stage3, stage4, grad,
):
    modes = probe.shape[0]

    @pl.loop(0, total.shape[2] // 16)
    def _(i):
        total[:, :, pl.ds(pl.multiple_of(i * 16, 16), 16), :] = jnp.zeros((2, total.shape[1], 16, LANES), F32)

    lane = lax.broadcasted_iota(jnp.int32, (W, LANES), 1)

    @pl.loop(0, count[0, 0])
    def _(slot):
        row = spots[0, 0, 0, slot]
        column = spots[0, 0, 1, slot]
        block = column // LANES
        shift = column - block * LANES
        back = lax.rem(LANES - shift, LANES)
        keep = lane < LANES - shift
        for part in range(2):
            rolled = []
            for i in range(3):
                x = ext[part, block + i, pl.ds(row, W), :]
                rolled.append(pltpu.roll(x, back, axis=1))
            for i in range(2):
                patch[part, :, i * LANES:(i + 1) * LANES] = jnp.where(keep, rolled[i], rolled[i + 1])

        step = 64
        for first in range(0, H, step):
            even, odd = [], []
            for m in range(modes):
                for half in range(2):
                    rows = pl.ds(half * H + first, step)
                    pr, pi = probe[m, 0, rows, :], probe[m, 1, rows, :]
                    xr, xi = patch[0, rows, :], patch[1, rows, :]
                    re = pr * xr - pi * xi
                    im = pr * xi + pi * xr
                    even.append(jnp.concatenate([re[:, :H] + re[:, H:], im[:, :H] + im[:, H:]], axis=1))
                    odd.append(jnp.concatenate([re[:, :H] - re[:, H:], im[:, :H] - im[:, H:]], axis=1))
            even = dot(jnp.concatenate(even, axis=0).astype(BF16), tables[0])
            odd = dot(jnp.concatenate(odd, axis=0).astype(BF16), tables[1])
            for m in range(modes):
                for n, h in enumerate((even, odd)):
                    low = h[(2 * m) * step:(2 * m + 1) * step]
                    high = h[(2 * m + 1) * step:(2 * m + 2) * step]
                    plus, minus = (low + high).astype(BF16), (low - high).astype(BF16)
                    for part in range(2):
                        rows = pl.ds(part * H + first, step)
                        columns = slice(part * H, (part + 1) * H)
                        stage2[m, 0, rows, n * H:(n + 1) * H] = plus[:, columns]
                        stage2[m, 1, rows, n * H:(n + 1) * H] = minus[:, columns]

        for n in range(2):
            for m in range(modes):
                wave[m, n] = dot(tables[2 + n], stage2[m, n])
            for first in range(0, H, 16):
                res = [wave[m, n, pl.ds(first, 16), :] for m in range(modes)]
                ims = [wave[m, n, pl.ds(H + first, 16), :] for m in range(modes)]
                inten = sum(x * x for x in res[1:] + ims) + res[0] * res[0]
                factor = 1.0 - root[slot, pl.ds(n * H + first, 16), :] / jnp.sqrt(inten + 1.0)
                for m in range(modes):
                    stage3[m, n, pl.ds(first, 16), :] = (factor * res[m]).astype(BF16)
                    stage3[m, n, pl.ds(H + first, 16), :] = (factor * ims[m]).astype(BF16)

        for m in range(modes):
            even = dot(tables[0], stage3[m, 0])
            odd = dot(tables[1], stage3[m, 1])
            plus, minus = (even + odd).astype(BF16), (even - odd).astype(BF16)
            for half, x in enumerate((plus, minus)):
                for part in range(2):
                    for n in range(2):
                        stage4[n, m, half * H:(half + 1) * H, part * H:(part + 1) * H] = x[part * H:(part + 1) * H, n * H:(n + 1) * H]

        step = 64
        for first in range(0, W, step):
            rows = pl.ds(first, step)
            even = dot(stage4[0, :, rows, :].reshape(modes * step, W), tables[2])
            odd = dot(stage4[1, :, rows, :].reshape(modes * step, W), tables[3])
            plus, minus = even + odd, even - odd
            for half, x in enumerate((plus, minus)):
                columns = slice(half * H, (half + 1) * H)
                gr = gi = None
                for m in range(modes):
                    pr, pi = probe[m, 0, rows, columns], probe[m, 1, rows, columns]
                    cr, ci = x[m * step:(m + 1) * step, :H], x[m * step:(m + 1) * step, H:]
                    re, im = pr * cr + pi * ci, pr * ci - pi * cr
                    gr, gi = (re, im) if gr is None else (gr + re, gi + im)
                grad[0, rows, columns] = gr
                grad[1, rows, columns] = gi

        moved = lane >= shift
        for part in range(2):
            left = pltpu.roll(grad[part, :, 0:LANES], shift, axis=1)
            right = pltpu.roll(grad[part, :, LANES:2 * LANES], shift, axis=1)
            zero = jnp.zeros_like(left)
            pieces = (jnp.where(moved, left, zero), jnp.where(moved, right, left), jnp.where(moved, zero, right))
            for i, piece in enumerate(pieces):
                where = (part, block + i, pl.ds(row, W), slice(None))
                total[where] = total[where] + piece


def frames_call(spots, count, probe, root, ext):
    modes = probe.shape[0]
    smem = pl.BlockSpec(memory_space=pltpu.SMEM)
    vmem = pl.BlockSpec(memory_space=pltpu.VMEM)
    return pl.pallas_call(
        frames_kernel,
        out_shape=jax.ShapeDtypeStruct(ext.shape, F32),
        in_specs=[smem, smem, vmem, vmem, vmem, vmem],
        out_specs=vmem,
        scratch_shapes=[
            pltpu.VMEM((2, W, W), F32),
            pltpu.VMEM((modes, 2, W, W), BF16),
            pltpu.VMEM((modes, 2, W, W), F32),
            pltpu.VMEM((modes, 2, W, W), BF16),
            pltpu.VMEM((2, modes, W, W), BF16),
            pltpu.VMEM((2, W, W), F32),
        ],
        compiler_params=pltpu.CompilerParams(vmem_limit_bytes=28 * 1024 * 1024),
        name="frames",
    )(spots, count, jnp.asarray(dft_tables()), probe, root, ext)


def body(mesh_shape, order, object_field, probe, positions, frame_count, measured):
    ext, root = halo_call(mesh_shape, order, object_field, measured[0, 0])
    total = frames_call(jnp.swapaxes(positions, 2, 3), frame_count, probe, root, ext)
    return sum_call(mesh_shape, order, total)


def solution(mesh):
    mesh_shape = (mesh.shape["gy"], mesh.shape["gx"])
    return jax.shard_map(
        functools.partial(body, mesh_shape, tuple(mesh.axis_names)),
        mesh=mesh,
        in_specs=(
            P(None, "gy", "gx"),
            P(),
            P("gy", "gx", None, None),
            P("gy", "gx"),
            P("gy", "gx", None, None, None),
        ),
        out_specs=P(None, "gy", "gx"),
        check_vma=False,
    )
```

```python
import functools
import math

import jax
import jax.numpy as jnp
import ml_dtypes
import numpy as np
from jax import lax
from jax.experimental import pallas as pl
from jax.experimental.pallas import tpu as pltpu
from jax.sharding import PartitionSpec as P

HALO = 128
W = 256
H = 128
LANES = 128
F32 = jnp.float32
BF16 = jnp.bfloat16
MESH = pl.DeviceIdType.MESH


def dft_tables():
    j = np.arange(H)[:, None]
    k = np.arange(H)[None, :]
    tables = []
    for odd in (0, 1):
        phase = 2.0 * math.pi / W * np.mod(j * (2 * k + odd), W)
        cosine = np.cos(phase) / math.sqrt(W)
        sine = np.sin(phase) / math.sqrt(W)
        tables.append(np.block([[cosine, -sine], [sine, cosine]]))
    tables += [tables[0].T, tables[1].T]
    return np.stack(tables).astype(ml_dtypes.bfloat16)


def dot(a, b):
    return jnp.dot(a, b, preferred_element_type=F32)


def neighbours(mesh_shape):
    ny, nx = mesh_shape
    y, x = lax.axis_index("gy"), lax.axis_index("gx")
    return y, x, dict(up=y > 0, down=y < ny - 1, left=x > 0, right=x < nx - 1)


def device(direction, y, x, mesh_shape):
    ny, nx = mesh_shape
    return {
        "up": (jnp.maximum(y - 1, 0), x),
        "down": (jnp.minimum(y + 1, ny - 1), x),
        "left": (y, jnp.maximum(x - 1, 0)),
        "right": (y, jnp.minimum(x + 1, nx - 1)),
    }[direction]


RELAYS = (("above", "last"), ("last", "below"), ("below", "first"), ("first", "above"))
NEXT = dict(above="below", below="above")
OPPOSITE = dict(up="down", down="up", left="right", right="left")


class Exchange:
    def __init__(self, mesh_shape, order, send, recv):
        self.shape, self.send, self.recv = mesh_shape, send, recv
        self.order = order
        self.y, self.x, self.has = neighbours(mesh_shape)
        ny = mesh_shape[0]
        self.rows = {"first": 0, "above": ny // 2 - 1, "below": ny // 2, "last": ny - 1}
        self.outer = (self.x < 2) | (self.x >= mesh_shape[1] - 2)
        self.copies = []

    def at(self, y, x):
        at = {"gy": y, "gx": x}
        return tuple(at[name] for name in self.order)

    def target(self, direction):
        return self.at(*device(direction, self.y, self.x, self.shape))

    def barrier(self):
        barrier = pltpu.get_barrier_semaphore()
        count = 0
        meets = [(there, self.target(direction)) for direction, there in self.has.items()]
        for a, b in RELAYS:
            for y, other in ((self.rows[a], self.rows[b]), (self.rows[b], self.rows[a])):
                meets.append((self.outer & (self.y == y), self.at(other, self.x)))
        for there, device in meets:
            count = count + there.astype(jnp.int32)

            @pl.when(there)
            def _():
                pl.semaphore_signal(barrier, inc=1, device_id=device, device_id_type=MESH)

        pl.semaphore_wait(barrier, count)

    def add(self, source, target, device, sends, receives):
        n = len(self.copies)
        descriptor = pltpu.make_async_remote_copy(
            src_ref=source, dst_ref=target, send_sem=self.send.at[n], recv_sem=self.recv.at[n],
            device_id=device, device_id_type=MESH,
        )
        self.copies.append((descriptor, sends, receives))
        return n

    def copy(self, direction, source, target, also=None, but=None):
        sends, receives = self.has[direction], self.has[OPPOSITE[direction]]
        if also is not None:
            sends, receives = sends & self.has[also], receives & self.has[also]
        if but is not None:
            inner = jnp.logical_not(self.outer)
            sends, receives = sends & (inner | (self.y != self.rows[but])), receives & (inner | (self.y != self.rows[NEXT[but]]))
        return self.add(source, target, self.target(direction), sends, receives)

    def relayed(self, a, b, c, source, buffer, target):
        first, by, last = self.rows[a], self.rows[b], self.rows[c]
        return (
            self.add(source, buffer, self.at(by, self.x), self.outer & (self.y == first), self.outer & (self.y == by)),
            self.add(buffer, target, self.at(last, self.x), self.outer & (self.y == by), self.outer & (self.y == last)),
        )

    def start(self, n):
        descriptor, sends, _ = self.copies[n]
        pl.when(sends)(descriptor.start)

    def arrived(self, n, then=None):
        descriptor, _, receives = self.copies[n]

        @pl.when(receives)
        def _():
            descriptor.wait_recv()
            if then is not None:
                then()

    def finish(self):
        for descriptor, sends, _ in self.copies:
            pl.when(sends)(descriptor.wait_send)


def halo_kernel(mesh_shape, order, field, measured, ext, root, values, perm, relay, send, recv, sem):
    tile = field.shape[1]
    slots = measured.shape[0]
    blocks = tile // LANES
    loads = [
        pltpu.make_async_copy(measured.at[:, :, pl.ds(i * LANES, LANES)], values.at[:, i], sem.at[i]) for i in range(2)
    ]
    net = Exchange(mesh_shape, order, send, recv)
    inside = pl.ds(HALO, tile)
    rows = {"up": (pl.ds(0, HALO), pl.ds(HALO + tile, HALO)), "down": (pl.ds(tile - HALO, HALO), pl.ds(0, HALO))}
    column = [pl.ds(i * LANES, LANES) for i in range(blocks)]
    inner = range(1, blocks - 1)
    crossing = {"down": ("above", "last", "below"), "up": ("below", "first", "above")}
    vertical, around = {}, []
    for i in (0, blocks - 1, *inner):
        for direction, (part, place) in rows.items():
            source, target = field.at[:, part, column[i]], ext.at[:, 1 + i, place, :]
            but = crossing[direction][0] if i in inner else None
            vertical[direction, i] = net.copy(direction, source, target, but=but)
            if i in inner:
                around.append(net.relayed(*crossing[direction], source, relay.at[:, len(around)], target))
    sides = [
        net.copy("left", field.at[:, :, column[0]], ext.at[:, 1 + blocks, inside, :]),
        net.copy("right", field.at[:, :, column[-1]], ext.at[:, 0, inside, :]),
    ]
    corners = []
    for direction, also in (("down", "up"), ("up", "down")):
        place = rows[direction][1]
        for i, block, towards, target in ((0, 1, "left", 1 + blocks), (blocks - 1, blocks, "right", 0)):
            n = net.copy(towards, ext.at[:, block, place, :], ext.at[:, target, place, :], also)
            corners.append((direction, i, n))

    net.barrier()
    for first, _ in around:
        net.start(first)
    for i in (0, blocks - 1):
        for direction in rows:
            net.start(vertical[direction, i])
    for n in sides:
        net.start(n)
    for i in inner:
        for direction in rows:
            net.start(vertical[direction, i])
    own = [pltpu.make_async_copy(field.at[:, :, column[i]], ext.at[:, 1 + i, inside, :], sem.at[2 + i]) for i in range(blocks)]
    for load in loads + own:
        load.start()

    def clear(there, blocks, first, count):
        @pl.when(jnp.logical_not(there))
        def _():
            for block in blocks:
                for part in range(2):
                    ext[part, block, first:first + count, :] = jnp.zeros((count, LANES), F32)

    has = net.has
    middle = range(1, 1 + blocks)
    clear(has["up"], middle, 0, HALO)
    clear(has["down"], middle, HALO + tile, HALO)
    for direction, block in (("left", 0), ("right", 1 + blocks)):
        clear(has[direction], (block,), HALO, tile)
        clear(has[direction] & has["up"], (block,), 0, HALO)
        clear(has[direction] & has["down"], (block,), HALO + tile, HALO)
    k = lax.broadcasted_iota(jnp.int32, (W, W), 0)
    perm[...] = (lax.broadcasted_iota(jnp.int32, (W, W), 1) == (k % 2) * H + k // 2).astype(F32).astype(BF16)
    for load in loads:
        load.wait()

    @pl.loop(0, slots)
    def _(slot):
        for half in range(2):
            x = jnp.sqrt(jnp.concatenate([values[slot, i, pl.ds(half, H, stride=2), :] for i in range(2)], axis=1))
            first = x.astype(BF16)
            x = x - first.astype(F32)
            second = x.astype(BF16)
            third = (x - second.astype(F32)).astype(BF16)
            root[slot, half * H:(half + 1) * H, :] = dot(first, perm[...]) + dot(second, perm[...]) + dot(third, perm[...])

    for load in own:
        load.wait()
    for first, second in around[:2]:
        net.arrived(first, lambda: net.start(second))
    for direction, i, n in corners:
        net.arrived(vertical[direction, i], lambda: net.start(n))
    for first, second in around[2:]:
        net.arrived(first, lambda: net.start(second))
    for n in sides:
        net.arrived(n)
    for _, second in around:
        net.arrived(second)
    for i in inner:
        for direction in rows:
            net.arrived(vertical[direction, i])
    for _, _, n in corners:
        net.arrived(n)
    net.finish()


def halo_call(mesh_shape, order, field, measured):
    tile = field.shape[1]
    side = tile + 2 * HALO
    hbm = pl.BlockSpec(memory_space=pltpu.HBM)
    vmem = pl.BlockSpec(memory_space=pltpu.VMEM)
    blocks = tile // LANES
    inner = blocks - 2
    n = 2 * blocks + 6 + 4 * inner
    return pl.pallas_call(
        functools.partial(halo_kernel, mesh_shape, order),
        out_shape=(
            jax.ShapeDtypeStruct((2, blocks + 3, side, LANES), F32),
            jax.ShapeDtypeStruct(measured.shape, F32),
        ),
        in_specs=[hbm, hbm],
        out_specs=(vmem, vmem),
        scratch_shapes=[
            pltpu.VMEM((measured.shape[0], 2, W, LANES), F32),
            pltpu.VMEM((W, W), BF16),
            pltpu.VMEM((2, 2 * inner, HALO, LANES), F32),
            pltpu.SemaphoreType.DMA((n,)),
            pltpu.SemaphoreType.DMA((n,)),
            pltpu.SemaphoreType.DMA((2 + blocks,)),
        ],
        compiler_params=pltpu.CompilerParams(collective_id=0, has_side_effects=True, vmem_limit_bytes=12 * 1024 * 1024),
        name="halo",
    )(pltpu.with_memory_space_constraint(field, pltpu.HBM), pltpu.with_memory_space_constraint(measured, pltpu.HBM))


def sum_kernel(mesh_shape, order, total, out, edges, from_left, from_right, from_up, from_down, send, recv):
    side = total.shape[2]
    tile = side - 2 * HALO
    blocks = tile // LANES
    net = Exchange(mesh_shape, order, send, recv)
    low, mid, high = pl.ds(0, HALO), pl.ds(HALO, tile), pl.ds(HALO + tile, HALO)
    across = {
        (direction, i): net.copy(direction, total.at[:, block, rows, :], target.at[:, rows, :])
        for i, rows in enumerate((low, high, mid))
        for direction, block, target in (("left", 0, from_right), ("right", blocks + 1, from_left))
    }
    crossing = {"down": ("above", "last", "below"), "up": ("below", "first", "above")}
    vertical, around = {}, {}
    for k, (direction, rows, target, relay) in enumerate((("up", low, from_down, from_up), ("down", high, from_up, from_down))):
        for i in range(1, blocks - 1):
            source, place = total.at[:, 1 + i, rows, :], target.at[:, i]
            vertical[direction, 1 + i] = net.copy(direction, source, place, but=crossing[direction][0])
            around[direction, 1 + i] = net.relayed(*crossing[direction], source, relay.at[:, i], place)
        for i, block in ((0, 0), (1, blocks - 1)):
            vertical[direction, i] = net.copy(direction, edges.at[k, i], target.at[:, block])

    net.barrier()
    for i in (0, 1):
        for direction in ("left", "right"):
            net.start(across[direction, i])
    for first, _ in around.values():
        net.start(first)
    for i in range(1, blocks - 1):
        for direction in ("up", "down"):
            net.start(vertical[direction, 1 + i])
    for direction in ("left", "right"):
        net.start(across[direction, 2])

    for i in range(blocks):
        out[:, :, i * LANES:(i + 1) * LANES] = total[:, 1 + i, HALO:HALO + tile, :]
    for k, rows in enumerate((low, high)):
        for i, block in ((0, 1), (1, blocks)):
            edges[k, i] = total[:, block, rows, :]

    early = [pair for (_, i), pair in around.items() if i == 2]
    for first, second in early:
        net.arrived(first, lambda: net.start(second))

    for k, (rows, direction) in enumerate(((low, "up"), (high, "down"))):
        for i, towards, source in ((0, "right", from_left), (1, "left", from_right)):
            def add():
                edges[k, i] = edges[k, i] + source[:, rows, :]

            net.arrived(across[towards, k], add)
            net.start(vertical[direction, i])

    for first, second in around.values():
        if (first, second) not in early:
            net.arrived(first, lambda: net.start(second))

    for i, towards, source in ((0, "right", from_left), (blocks - 1, "left", from_right)):
        def add():
            columns = slice(i * LANES, (i + 1) * LANES)
            out[:, :, columns] = out[:, :, columns] + source[:, mid, :]

        net.arrived(across[towards, 2], add)

    for i, part in (*((1 + part, part) for part in range(1, blocks - 1)), (0, 0), (1, blocks - 1)):
        for towards, first, source in (("down", 0, from_up), ("up", tile - HALO, from_down)):
            def add():
                place = (slice(None), slice(first, first + HALO), slice(part * LANES, (part + 1) * LANES))
                out[place] = out[place] + source[:, part]

            net.arrived(vertical[towards, i], add)
            if i > 1:
                net.arrived(around[towards, i][1], add)
    net.finish()


def sum_call(mesh_shape, order, total):
    side = total.shape[2]
    tile = side - 2 * HALO
    blocks = tile // LANES
    n = 6 + 2 * blocks + 4 * (blocks - 2)
    vmem = pl.BlockSpec(memory_space=pltpu.VMEM)
    return pl.pallas_call(
        functools.partial(sum_kernel, mesh_shape, order),
        out_shape=jax.ShapeDtypeStruct((2, tile, tile), F32),
        in_specs=[vmem],
        out_specs=vmem,
        scratch_shapes=[
            pltpu.VMEM((2, 2, 2, HALO, LANES), F32),
            pltpu.VMEM((2, side, LANES), F32),
            pltpu.VMEM((2, side, LANES), F32),
            pltpu.VMEM((2, blocks, HALO, LANES), F32),
            pltpu.VMEM((2, blocks, HALO, LANES), F32),
            pltpu.SemaphoreType.DMA((n,)),
            pltpu.SemaphoreType.DMA((n,)),
        ],
        compiler_params=pltpu.CompilerParams(collective_id=1, has_side_effects=True, vmem_limit_bytes=16 * 1024 * 1024),
        name="sums",
    )(total)


def frames_kernel(
    spots, count, tables, probe, root, ext,
    total,
    patch, stage2, wave, stage3, stage4, grad,
):
    modes = probe.shape[0]

    @pl.loop(0, total.shape[2] // 16)
    def _(i):
        total[:, :, pl.ds(pl.multiple_of(i * 16, 16), 16), :] = jnp.zeros((2, total.shape[1], 16, LANES), F32)

    lane = lax.broadcasted_iota(jnp.int32, (W, LANES), 1)

    @pl.loop(0, count[0, 0])
    def _(slot):
        row = spots[0, 0, 0, slot]
        column = spots[0, 0, 1, slot]
        block = column // LANES
        shift = column - block * LANES
        back = lax.rem(LANES - shift, LANES)
        keep = lane < LANES - shift
        for part in range(2):
            rolled = []
            for i in range(3):
                x = ext[part, block + i, pl.ds(row, W), :]
                rolled.append(pltpu.roll(x, back, axis=1))
            for i in range(2):
                patch[part, :, i * LANES:(i + 1) * LANES] = jnp.where(keep, rolled[i], rolled[i + 1])

        step = 64
        for first in range(0, H, step):
            even, odd = [], []
            for m in range(modes):
                for half in range(2):
                    rows = pl.ds(half * H + first, step)
                    pr, pi = probe[m, 0, rows, :], probe[m, 1, rows, :]
                    xr, xi = patch[0, rows, :], patch[1, rows, :]
                    re = pr * xr - pi * xi
                    im = pr * xi + pi * xr
                    even.append(jnp.concatenate([re[:, :H] + re[:, H:], im[:, :H] + im[:, H:]], axis=1))
                    odd.append(jnp.concatenate([re[:, :H] - re[:, H:], im[:, :H] - im[:, H:]], axis=1))
            even = dot(jnp.concatenate(even, axis=0).astype(BF16), tables[0])
            odd = dot(jnp.concatenate(odd, axis=0).astype(BF16), tables[1])
            for m in range(modes):
                for n, h in enumerate((even, odd)):
                    low = h[(2 * m) * step:(2 * m + 1) * step]
                    high = h[(2 * m + 1) * step:(2 * m + 2) * step]
                    plus, minus = (low + high).astype(BF16), (low - high).astype(BF16)
                    for part in range(2):
                        rows = pl.ds(part * H + first, step)
                        columns = slice(part * H, (part + 1) * H)
                        stage2[m, 0, rows, n * H:(n + 1) * H] = plus[:, columns]
                        stage2[m, 1, rows, n * H:(n + 1) * H] = minus[:, columns]

        for n in range(2):
            for m in range(modes):
                wave[m, n] = dot(tables[2 + n], stage2[m, n])
            for first in range(0, H, 16):
                res = [wave[m, n, pl.ds(first, 16), :] for m in range(modes)]
                ims = [wave[m, n, pl.ds(H + first, 16), :] for m in range(modes)]
                inten = sum(x * x for x in res[1:] + ims) + res[0] * res[0]
                factor = 1.0 - root[slot, pl.ds(n * H + first, 16), :] / jnp.sqrt(inten + 1.0)
                for m in range(modes):
                    stage3[m, n, pl.ds(first, 16), :] = (factor * res[m]).astype(BF16)
                    stage3[m, n, pl.ds(H + first, 16), :] = (factor * ims[m]).astype(BF16)

        for m in range(modes):
            even = dot(tables[0], stage3[m, 0])
            odd = dot(tables[1], stage3[m, 1])
            plus, minus = (even + odd).astype(BF16), (even - odd).astype(BF16)
            for half, x in enumerate((plus, minus)):
                for part in range(2):
                    for n in range(2):
                        stage4[n, m, half * H:(half + 1) * H, part * H:(part + 1) * H] = x[part * H:(part + 1) * H, n * H:(n + 1) * H]

        step = 64
        for first in range(0, W, step):
            rows = pl.ds(first, step)
            even = dot(stage4[0, :, rows, :].reshape(modes * step, W), tables[2])
            odd = dot(stage4[1, :, rows, :].reshape(modes * step, W), tables[3])
            plus, minus = even + odd, even - odd
            for half, x in enumerate((plus, minus)):
                columns = slice(half * H, (half + 1) * H)
                gr = gi = None
                for m in range(modes):
                    pr, pi = probe[m, 0, rows, columns], probe[m, 1, rows, columns]
                    cr, ci = x[m * step:(m + 1) * step, :H], x[m * step:(m + 1) * step, H:]
                    re, im = pr * cr + pi * ci, pr * ci - pi * cr
                    gr, gi = (re, im) if gr is None else (gr + re, gi + im)
                grad[0, rows, columns] = gr
                grad[1, rows, columns] = gi

        moved = lane >= shift
        for part in range(2):
            left = pltpu.roll(grad[part, :, 0:LANES], shift, axis=1)
            right = pltpu.roll(grad[part, :, LANES:2 * LANES], shift, axis=1)
            zero = jnp.zeros_like(left)
            pieces = (jnp.where(moved, left, zero), jnp.where(moved, right, left), jnp.where(moved, zero, right))
            for i, piece in enumerate(pieces):
                where = (part, block + i, pl.ds(row, W), slice(None))
                total[where] = total[where] + piece


def frames_call(spots, count, probe, root, ext):
    modes = probe.shape[0]
    smem = pl.BlockSpec(memory_space=pltpu.SMEM)
    vmem = pl.BlockSpec(memory_space=pltpu.VMEM)
    return pl.pallas_call(
        frames_kernel,
        out_shape=jax.ShapeDtypeStruct(ext.shape, F32),
        in_specs=[smem, smem, vmem, vmem, vmem, vmem],
        out_specs=vmem,
        scratch_shapes=[
            pltpu.VMEM((2, W, W), F32),
            pltpu.VMEM((modes, 2, W, W), BF16),
            pltpu.VMEM((modes, 2, W, W), F32),
            pltpu.VMEM((modes, 2, W, W), BF16),
            pltpu.VMEM((2, modes, W, W), BF16),
            pltpu.VMEM((2, W, W), F32),
        ],
        compiler_params=pltpu.CompilerParams(vmem_limit_bytes=28 * 1024 * 1024),
        name="frames",
    )(spots, count, jnp.asarray(dft_tables()), probe, root, ext)


def body(mesh_shape, order, object_field, probe, positions, frame_count, measured):
    ext, root = halo_call(mesh_shape, order, object_field, measured[0, 0])
    total = frames_call(jnp.swapaxes(positions, 2, 3), frame_count, probe, root, ext)
    return sum_call(mesh_shape, order, total)


def solution(mesh):
    mesh_shape = (mesh.shape["gy"], mesh.shape["gx"])
    return jax.shard_map(
        functools.partial(body, mesh_shape, tuple(mesh.axis_names)),
        mesh=mesh,
        in_specs=(
            P(None, "gy", "gx"),
            P(),
            P("gy", "gx", None, None),
            P("gy", "gx"),
            P("gy", "gx", None, None, None),
        ),
        out_specs=P(None, "gy", "gx"),
        check_vma=False,
    )
```

```python
import functools
import math

import jax
import jax.numpy as jnp
import ml_dtypes
import numpy as np
from jax import lax
from jax.experimental import pallas as pl
from jax.experimental.pallas import tpu as pltpu
from jax.sharding import PartitionSpec as P

HALO = 128
W = 256
H = 128
LANES = 128
F32 = jnp.float32
BF16 = jnp.bfloat16
MESH = pl.DeviceIdType.MESH


def dft_tables():
    j = np.arange(H)[:, None]
    k = np.arange(H)[None, :]
    tables = []
    for odd in (0, 1):
        phase = 2.0 * math.pi / W * np.mod(j * (2 * k + odd), W)
        cosine = np.cos(phase) / math.sqrt(W)
        sine = np.sin(phase) / math.sqrt(W)
        tables.append(np.block([[cosine, -sine], [sine, cosine]]))
    tables += [tables[0].T, tables[1].T]
    return np.stack(tables).astype(ml_dtypes.bfloat16)


def dot(a, b):
    return jnp.dot(a, b, preferred_element_type=F32)


def neighbours(mesh_shape):
    ny, nx = mesh_shape
    y, x = lax.axis_index("gy"), lax.axis_index("gx")
    return y, x, dict(up=y > 0, down=y < ny - 1, left=x > 0, right=x < nx - 1)


def device(direction, y, x, mesh_shape):
    ny, nx = mesh_shape
    return {
        "up": (jnp.maximum(y - 1, 0), x),
        "down": (jnp.minimum(y + 1, ny - 1), x),
        "left": (y, jnp.maximum(x - 1, 0)),
        "right": (y, jnp.minimum(x + 1, nx - 1)),
    }[direction]


OPPOSITE = dict(up="down", down="up", left="right", right="left")


class Exchange:
    def __init__(self, mesh_shape, order, send, recv):
        self.shape, self.send, self.recv = mesh_shape, send, recv
        self.order = order
        self.y, self.x, self.has = neighbours(mesh_shape)
        ny = mesh_shape[0]
        first, above, below, last = 0, ny // 2 - 1, ny // 2, ny - 1
        self.edge = {"first": self.y == first, "last": self.y == last}
        self.by = {"first": self.y == below, "last": self.y == above}
        self.away = jnp.where(self.edge["first"], below, above)
        self.back = jnp.where(self.by["first"], first, last)
        middle = mesh_shape[1] // 2
        self.ways = {"right": (middle - 1, mesh_shape[1] - 1, middle), "left": (middle, 0, middle - 1)}
        self.copies = []

    def at(self, y, x):
        at = {"gy": y, "gx": x}
        return tuple(at[name] for name in self.order)

    def target(self, direction):
        return self.at(*device(direction, self.y, self.x, self.shape))

    def barrier(self):
        barrier = pltpu.get_barrier_semaphore()
        count = 0
        meets = [(there, self.target(direction)) for direction, there in self.has.items()]
        edge, by = self.edge["first"] | self.edge["last"], self.by["first"] | self.by["last"]
        for source, relay, target in self.ways.values():
            for column in (source, target):
                meets.append((edge & (self.x == column), self.at(self.away, relay)))
                meets.append((by & (self.x == relay), self.at(self.back, column)))
        for there, device in meets:
            count = count + there.astype(jnp.int32)

            @pl.when(there)
            def _():
                pl.semaphore_signal(barrier, inc=1, device_id=device, device_id_type=MESH)

        pl.semaphore_wait(barrier, count)

    def add(self, source, target, device, sends, receives):
        n = len(self.copies)
        descriptor = pltpu.make_async_remote_copy(
            src_ref=source, dst_ref=target, send_sem=self.send.at[n], recv_sem=self.recv.at[n],
            device_id=device, device_id_type=MESH,
        )
        self.copies.append((descriptor, sends, receives))
        return n

    def copy(self, direction, source, target, also=None):
        sends, receives = self.has[direction], self.has[OPPOSITE[direction]]
        if also is not None:
            sends, receives = sends & self.has[also], receives & self.has[also]
        if direction in self.ways:
            first, _, last = self.ways[direction]
            inside = jnp.logical_not(self.edge["first"] | self.edge["last"])
            sends, receives = sends & (inside | (self.x != first)), receives & (inside | (self.x != last))
        return self.add(source, target, self.target(direction), sends, receives)

    def detour(self, direction, source, buffer, target, rows=("first", "last")):
        first, relay, last = self.ways[direction]
        edge, by = (functools.reduce(jnp.logical_or, [flags[row] for row in rows]) for flags in (self.edge, self.by))
        by = by & (self.x == relay)
        return (
            self.add(source, buffer, self.at(self.away, relay), edge & (self.x == first), by),
            self.add(buffer, target, self.at(self.back, last), by, edge & (self.x == last)),
        )

    def start(self, n):
        descriptor, sends, _ = self.copies[n]
        pl.when(sends)(descriptor.start)

    def arrived(self, n, then=None):
        descriptor, _, receives = self.copies[n]

        @pl.when(receives)
        def _():
            descriptor.wait_recv()
            if then is not None:
                then()

    def finish(self):
        for descriptor, sends, _ in self.copies:
            pl.when(sends)(descriptor.wait_send)


def halo_kernel(mesh_shape, order, field, measured, ext, root, values, perm, relay, send, recv, sem):
    tile = field.shape[1]
    slots = measured.shape[0]
    blocks = tile // LANES
    loads = [
        pltpu.make_async_copy(measured.at[:, :, pl.ds(i * LANES, LANES)], values.at[:, i], sem.at[i]) for i in range(2)
    ]
    net = Exchange(mesh_shape, order, send, recv)
    inside = pl.ds(HALO, tile)
    rows = {"up": (pl.ds(0, HALO), pl.ds(HALO + tile, HALO)), "down": (pl.ds(tile - HALO, HALO), pl.ds(0, HALO))}
    column = [pl.ds(i * LANES, LANES) for i in range(blocks)]
    inner = range(1, blocks - 1)
    vertical = {}
    for i in (0, blocks - 1, *inner):
        for direction, (part, place) in rows.items():
            vertical[direction, i] = net.copy(direction, field.at[:, part, column[i]], ext.at[:, 1 + i, place, :])
    sides = [
        net.copy("left", field.at[:, :, column[0]], ext.at[:, 1 + blocks, inside, :]),
        net.copy("right", field.at[:, :, column[-1]], ext.at[:, 0, inside, :]),
    ]
    strips = []
    for k in range(0, tile, tile // 2):
        part, place = pl.ds(k, tile // 2), pl.ds(HALO + k, tile // 2)
        for towards, i, target in (("left", 0, 1 + blocks), ("right", blocks - 1, 0)):
            strips.append(net.detour(towards, field.at[:, part, column[i]], relay.at[:, part, :], ext.at[:, target, place, :]))
    corners, turns = [], []
    for direction, also, edge in (("down", "up", "last"), ("up", "down", "first")):
        place = rows[direction][1]
        for i, block, towards, target in ((0, 1, "left", 1 + blocks), (blocks - 1, blocks, "right", 0)):
            source, target = ext.at[:, block, place, :], ext.at[:, target, place, :]
            n = net.copy(towards, source, target, also)
            turn = net.detour(towards, source, relay.at[:, pl.ds(tile, HALO), :], target, (edge,))
            corners.append((direction, i, n, turn[0]))
            turns.append(turn)

    net.barrier()
    for first, _ in strips:
        net.start(first)
    for i in (0, blocks - 1):
        for direction in rows:
            net.start(vertical[direction, i])
    for n in sides:
        net.start(n)
    for i in inner:
        for direction in rows:
            net.start(vertical[direction, i])
    own = [pltpu.make_async_copy(field.at[:, :, column[i]], ext.at[:, 1 + i, inside, :], sem.at[2 + i]) for i in range(blocks)]
    for load in loads + own:
        load.start()

    def clear(there, blocks, first, count):
        @pl.when(jnp.logical_not(there))
        def _():
            for block in blocks:
                for part in range(2):
                    ext[part, block, first:first + count, :] = jnp.zeros((count, LANES), F32)

    has = net.has
    middle = range(1, 1 + blocks)
    clear(has["up"], middle, 0, HALO)
    clear(has["down"], middle, HALO + tile, HALO)
    for direction, block in (("left", 0), ("right", 1 + blocks)):
        clear(has[direction], (block,), HALO, tile)
        clear(has[direction] & has["up"], (block,), 0, HALO)
        clear(has[direction] & has["down"], (block,), HALO + tile, HALO)
    k = lax.broadcasted_iota(jnp.int32, (W, W), 0)
    perm[...] = (lax.broadcasted_iota(jnp.int32, (W, W), 1) == (k % 2) * H + k // 2).astype(F32).astype(BF16)
    for load in loads:
        load.wait()

    @pl.loop(0, slots)
    def _(slot):
        for half in range(2):
            x = jnp.sqrt(jnp.concatenate([values[slot, i, pl.ds(half, H, stride=2), :] for i in range(2)], axis=1))
            first = x.astype(BF16)
            x = x - first.astype(F32)
            second = x.astype(BF16)
            third = (x - second.astype(F32)).astype(BF16)
            root[slot, half * H:(half + 1) * H, :] = dot(first, perm[...]) + dot(second, perm[...]) + dot(third, perm[...])

    for load in own:
        load.wait()
    def forward(pairs):
        for first, second in pairs:
            net.arrived(first, lambda: net.start(second))

    forward(strips)
    for direction, i, n, turn in corners:
        def send():
            net.start(n)
            net.start(turn)

        net.arrived(vertical[direction, i], send)
    for n in sides:
        net.arrived(n)
    forward(turns)
    for i in inner:
        for direction in rows:
            net.arrived(vertical[direction, i])
    for _, second in strips + turns:
        net.arrived(second)
    for _, _, n, _ in corners:
        net.arrived(n)
    net.finish()


def halo_call(mesh_shape, order, field, measured):
    tile = field.shape[1]
    side = tile + 2 * HALO
    hbm = pl.BlockSpec(memory_space=pltpu.HBM)
    vmem = pl.BlockSpec(memory_space=pltpu.VMEM)
    blocks = tile // LANES
    n = 2 * blocks + 6 + 16
    return pl.pallas_call(
        functools.partial(halo_kernel, mesh_shape, order),
        out_shape=(
            jax.ShapeDtypeStruct((2, blocks + 3, side, LANES), F32),
            jax.ShapeDtypeStruct(measured.shape, F32),
        ),
        in_specs=[hbm, hbm],
        out_specs=(vmem, vmem),
        scratch_shapes=[
            pltpu.VMEM((measured.shape[0], 2, W, LANES), F32),
            pltpu.VMEM((W, W), BF16),
            pltpu.VMEM((2, tile + HALO, LANES), F32),
            pltpu.SemaphoreType.DMA((n,)),
            pltpu.SemaphoreType.DMA((n,)),
            pltpu.SemaphoreType.DMA((2 + blocks,)),
        ],
        compiler_params=pltpu.CompilerParams(collective_id=0, has_side_effects=True, vmem_limit_bytes=12 * 1024 * 1024),
        name="halo",
    )(pltpu.with_memory_space_constraint(field, pltpu.HBM), pltpu.with_memory_space_constraint(measured, pltpu.HBM))


def sum_kernel(mesh_shape, order, total, out, edges, from_left, from_right, from_up, from_down, send, recv):
    side = total.shape[2]
    tile = side - 2 * HALO
    blocks = tile // LANES
    net = Exchange(mesh_shape, order, send, recv)
    low, mid, high = pl.ds(0, HALO), pl.ds(HALO, tile), pl.ds(HALO + tile, HALO)
    across = {
        (direction, i): net.copy(direction, total.at[:, block, rows, :], target.at[:, rows, :])
        for i, rows in enumerate((low, high, mid))
        for direction, block, target in (("left", 0, from_right), ("right", blocks + 1, from_left))
    }
    strips, turns = [], {}
    for direction, block, target, relay in (("left", 0, from_right, from_left), ("right", blocks + 1, from_left, from_right)):
        def part(rows):
            return total.at[:, block, rows, :], relay.at[:, rows, :], target.at[:, rows, :]

        for k in range(HALO, HALO + tile, tile // 2):
            strips.append((direction, net.detour(direction, *part(pl.ds(k, tile // 2)))))
        for k, rows, edge in ((0, low, "last"), (1, high, "first")):
            turns[direction, k] = net.detour(direction, *part(rows), (edge,))
    vertical = {}
    for k, (direction, rows, target) in enumerate((("up", low, from_down), ("down", high, from_up))):
        for i in range(1, blocks - 1):
            vertical[direction, 1 + i] = net.copy(direction, total.at[:, 1 + i, rows, :], target.at[:, i])
        for i, block in ((0, 0), (1, blocks - 1)):
            vertical[direction, i] = net.copy(direction, edges.at[k, i], target.at[:, block])

    net.barrier()
    for i in (0, 1):
        for direction in ("left", "right"):
            net.start(across[direction, i])
    for first, _ in (*turns.values(), *(pair for _, pair in strips)):
        net.start(first)
    for i in range(1, blocks - 1):
        for direction in ("up", "down"):
            net.start(vertical[direction, 1 + i])
    for direction in ("left", "right"):
        net.start(across[direction, 2])

    for i in range(blocks):
        out[:, :, i * LANES:(i + 1) * LANES] = total[:, 1 + i, HALO:HALO + tile, :]
    for k, rows in enumerate((low, high)):
        for i, block in ((0, 1), (1, blocks)):
            edges[k, i] = total[:, block, rows, :]

    for first, second in (*turns.values(), *(pair for _, pair in strips)):
        net.arrived(first, lambda: net.start(second))

    for k, (rows, direction) in enumerate(((low, "up"), (high, "down"))):
        for i, towards, source in ((0, "right", from_left), (1, "left", from_right)):
            def add():
                edges[k, i] = edges[k, i] + source[:, rows, :]

            net.arrived(across[towards, k], add)
            net.arrived(turns[towards, k][1], add)
            net.start(vertical[direction, i])

    for i, towards, source in ((0, "right", from_left), (blocks - 1, "left", from_right)):
        waits = []

        def add():
            columns = slice(i * LANES, (i + 1) * LANES)
            out[:, :, columns] = out[:, :, columns] + source[:, mid, :]

        net.arrived(across[towards, 2], add)
        for direction, (_, second) in strips:
            if direction == towards:
                waits.append(second)
        last = waits.pop()
        for second in waits:
            net.arrived(second)
        net.arrived(last, add)

    for i, part in (*((1 + part, part) for part in range(1, blocks - 1)), (0, 0), (1, blocks - 1)):
        for towards, first, source in (("down", 0, from_up), ("up", tile - HALO, from_down)):
            def add():
                place = (slice(None), slice(first, first + HALO), slice(part * LANES, (part + 1) * LANES))
                out[place] = out[place] + source[:, part]

            net.arrived(vertical[towards, i], add)
    net.finish()


def sum_call(mesh_shape, order, total):
    side = total.shape[2]
    tile = side - 2 * HALO
    blocks = tile // LANES
    n = 6 + 2 * blocks + 16
    vmem = pl.BlockSpec(memory_space=pltpu.VMEM)
    return pl.pallas_call(
        functools.partial(sum_kernel, mesh_shape, order),
        out_shape=jax.ShapeDtypeStruct((2, tile, tile), F32),
        in_specs=[vmem],
        out_specs=vmem,
        scratch_shapes=[
            pltpu.VMEM((2, 2, 2, HALO, LANES), F32),
            pltpu.VMEM((2, side, LANES), F32),
            pltpu.VMEM((2, side, LANES), F32),
            pltpu.VMEM((2, blocks, HALO, LANES), F32),
            pltpu.VMEM((2, blocks, HALO, LANES), F32),
            pltpu.SemaphoreType.DMA((n,)),
            pltpu.SemaphoreType.DMA((n,)),
        ],
        compiler_params=pltpu.CompilerParams(collective_id=1, has_side_effects=True, vmem_limit_bytes=16 * 1024 * 1024),
        name="sums",
    )(total)


def frames_kernel(
    spots, count, tables, probe, root, ext,
    total,
    patch, stage2, wave, stage3, stage4, grad,
):
    modes = probe.shape[0]

    @pl.loop(0, total.shape[2] // 16)
    def _(i):
        total[:, :, pl.ds(pl.multiple_of(i * 16, 16), 16), :] = jnp.zeros((2, total.shape[1], 16, LANES), F32)

    lane = lax.broadcasted_iota(jnp.int32, (W, LANES), 1)

    @pl.loop(0, count[0, 0])
    def _(slot):
        row = spots[0, 0, 0, slot]
        column = spots[0, 0, 1, slot]
        block = column // LANES
        shift = column - block * LANES
        back = lax.rem(LANES - shift, LANES)
        keep = lane < LANES - shift
        for part in range(2):
            rolled = []
            for i in range(3):
                x = ext[part, block + i, pl.ds(row, W), :]
                rolled.append(pltpu.roll(x, back, axis=1))
            for i in range(2):
                patch[part, :, i * LANES:(i + 1) * LANES] = jnp.where(keep, rolled[i], rolled[i + 1])

        step = 64
        for first in range(0, H, step):
            even, odd = [], []
            for m in range(modes):
                for half in range(2):
                    rows = pl.ds(half * H + first, step)
                    pr, pi = probe[m, 0, rows, :], probe[m, 1, rows, :]
                    xr, xi = patch[0, rows, :], patch[1, rows, :]
                    re = pr * xr - pi * xi
                    im = pr * xi + pi * xr
                    even.append(jnp.concatenate([re[:, :H] + re[:, H:], im[:, :H] + im[:, H:]], axis=1))
                    odd.append(jnp.concatenate([re[:, :H] - re[:, H:], im[:, :H] - im[:, H:]], axis=1))
            even = dot(jnp.concatenate(even, axis=0).astype(BF16), tables[0])
            odd = dot(jnp.concatenate(odd, axis=0).astype(BF16), tables[1])
            for m in range(modes):
                for n, h in enumerate((even, odd)):
                    low = h[(2 * m) * step:(2 * m + 1) * step]
                    high = h[(2 * m + 1) * step:(2 * m + 2) * step]
                    plus, minus = (low + high).astype(BF16), (low - high).astype(BF16)
                    for part in range(2):
                        rows = pl.ds(part * H + first, step)
                        columns = slice(part * H, (part + 1) * H)
                        stage2[m, 0, rows, n * H:(n + 1) * H] = plus[:, columns]
                        stage2[m, 1, rows, n * H:(n + 1) * H] = minus[:, columns]

        for n in range(2):
            for m in range(modes):
                wave[m, n] = dot(tables[2 + n], stage2[m, n])
            for first in range(0, H, 16):
                res = [wave[m, n, pl.ds(first, 16), :] for m in range(modes)]
                ims = [wave[m, n, pl.ds(H + first, 16), :] for m in range(modes)]
                inten = sum(x * x for x in res[1:] + ims) + res[0] * res[0]
                factor = 1.0 - root[slot, pl.ds(n * H + first, 16), :] * lax.rsqrt(inten + 1.0)
                for m in range(modes):
                    stage3[m, n, pl.ds(first, 16), :] = (factor * res[m]).astype(BF16)
                    stage3[m, n, pl.ds(H + first, 16), :] = (factor * ims[m]).astype(BF16)

        for m in range(modes):
            even = dot(tables[0], stage3[m, 0])
            odd = dot(tables[1], stage3[m, 1])
            plus, minus = (even + odd).astype(BF16), (even - odd).astype(BF16)
            for half, x in enumerate((plus, minus)):
                for part in range(2):
                    for n in range(2):
                        stage4[n, m, half * H:(half + 1) * H, part * H:(part + 1) * H] = x[part * H:(part + 1) * H, n * H:(n + 1) * H]

        step = 64
        for first in range(0, W, step):
            rows = pl.ds(first, step)
            even = dot(stage4[0, :, rows, :].reshape(modes * step, W), tables[2])
            odd = dot(stage4[1, :, rows, :].reshape(modes * step, W), tables[3])
            plus, minus = even + odd, even - odd
            for half, x in enumerate((plus, minus)):
                columns = slice(half * H, (half + 1) * H)
                gr = gi = None
                for m in range(modes):
                    pr, pi = probe[m, 0, rows, columns], probe[m, 1, rows, columns]
                    cr, ci = x[m * step:(m + 1) * step, :H], x[m * step:(m + 1) * step, H:]
                    re, im = pr * cr + pi * ci, pr * ci - pi * cr
                    gr, gi = (re, im) if gr is None else (gr + re, gi + im)
                grad[0, rows, columns] = gr
                grad[1, rows, columns] = gi

        moved = lane >= shift
        for part in range(2):
            left = pltpu.roll(grad[part, :, 0:LANES], shift, axis=1)
            right = pltpu.roll(grad[part, :, LANES:2 * LANES], shift, axis=1)
            zero = jnp.zeros_like(left)
            pieces = (jnp.where(moved, left, zero), jnp.where(moved, right, left), jnp.where(moved, zero, right))
            for i, piece in enumerate(pieces):
                where = (part, block + i, pl.ds(row, W), slice(None))
                total[where] = total[where] + piece


def frames_call(spots, count, probe, root, ext):
    modes = probe.shape[0]
    smem = pl.BlockSpec(memory_space=pltpu.SMEM)
    vmem = pl.BlockSpec(memory_space=pltpu.VMEM)
    return pl.pallas_call(
        frames_kernel,
        out_shape=jax.ShapeDtypeStruct(ext.shape, F32),
        in_specs=[smem, smem, vmem, vmem, vmem, vmem],
        out_specs=vmem,
        scratch_shapes=[
            pltpu.VMEM((2, W, W), F32),
            pltpu.VMEM((modes, 2, W, W), BF16),
            pltpu.VMEM((modes, 2, W, W), F32),
            pltpu.VMEM((modes, 2, W, W), BF16),
            pltpu.VMEM((2, modes, W, W), BF16),
            pltpu.VMEM((2, W, W), F32),
        ],
        compiler_params=pltpu.CompilerParams(vmem_limit_bytes=28 * 1024 * 1024),
        name="frames",
    )(spots, count, jnp.asarray(dft_tables()), probe, root, ext)


def body(mesh_shape, order, object_field, probe, positions, frame_count, measured):
    ext, root = halo_call(mesh_shape, order, object_field, measured[0, 0])
    total = frames_call(jnp.swapaxes(positions, 2, 3), frame_count, probe, root, ext)
    return sum_call(mesh_shape, order, total)


def solution(mesh):
    mesh_shape = (mesh.shape["gy"], mesh.shape["gx"])
    return jax.shard_map(
        functools.partial(body, mesh_shape, tuple(mesh.axis_names)),
        mesh=mesh,
        in_specs=(
            P(None, "gy", "gx"),
            P(),
            P("gy", "gx", None, None),
            P("gy", "gx"),
            P("gy", "gx", None, None, None),
        ),
        out_specs=P(None, "gy", "gx"),
        check_vma=False,
    )
```

```python
import functools
import math

import jax
import jax.numpy as jnp
import ml_dtypes
import numpy as np
from jax import lax
from jax.experimental import pallas as pl
from jax.experimental.pallas import tpu as pltpu
from jax.sharding import PartitionSpec as P

HALO = 128
W = 256
H = 128
LANES = 128
F32 = jnp.float32
BF16 = jnp.bfloat16
MESH = pl.DeviceIdType.MESH


def dft_tables():
    j = np.arange(H)[:, None]
    k = np.arange(H)[None, :]
    tables = []
    for odd in (0, 1):
        phase = 2.0 * math.pi / W * np.mod(j * (2 * k + odd), W)
        cosine = np.cos(phase) / math.sqrt(W)
        sine = np.sin(phase) / math.sqrt(W)
        tables.append(np.block([[cosine, -sine], [sine, cosine]]))
    tables += [tables[0].T, tables[1].T]
    return np.stack(tables).astype(ml_dtypes.bfloat16)


def dot(a, b):
    return jnp.dot(a, b, preferred_element_type=F32)


def neighbours(mesh_shape):
    ny, nx = mesh_shape
    y, x = lax.axis_index("gy"), lax.axis_index("gx")
    return y, x, dict(up=y > 0, down=y < ny - 1, left=x > 0, right=x < nx - 1)


def device(direction, y, x, mesh_shape):
    ny, nx = mesh_shape
    return {
        "up": (jnp.maximum(y - 1, 0), x),
        "down": (jnp.minimum(y + 1, ny - 1), x),
        "left": (y, jnp.maximum(x - 1, 0)),
        "right": (y, jnp.minimum(x + 1, nx - 1)),
    }[direction]


OPPOSITE = dict(up="down", down="up", left="right", right="left")


class Exchange:
    def __init__(self, mesh_shape, order, send, recv):
        self.shape, self.send, self.recv = mesh_shape, send, recv
        self.order = order
        self.y, self.x, self.has = neighbours(mesh_shape)
        ny = mesh_shape[0]
        first, above, below, last = 0, ny // 2 - 1, ny // 2, ny - 1
        self.edge = {"first": self.y == first, "last": self.y == last}
        self.by = {"first": self.y == below, "last": self.y == above}
        self.away = jnp.where(self.edge["first"], below, above)
        self.back = jnp.where(self.by["first"], first, last)
        middle = mesh_shape[1] // 2
        self.ways = {"right": (middle - 1, mesh_shape[1] - 1, middle), "left": (middle, 0, middle - 1)}
        self.copies = []

    def at(self, y, x):
        at = {"gy": y, "gx": x}
        return tuple(at[name] for name in self.order)

    def target(self, direction):
        return self.at(*device(direction, self.y, self.x, self.shape))

    def barrier(self):
        barrier = pltpu.get_barrier_semaphore()
        count = 0
        meets = [(there, self.target(direction)) for direction, there in self.has.items()]
        edge, by = self.edge["first"] | self.edge["last"], self.by["first"] | self.by["last"]
        for source, relay, target in self.ways.values():
            for column in (source, target):
                meets.append((edge & (self.x == column), self.at(self.away, relay)))
                meets.append((by & (self.x == relay), self.at(self.back, column)))
        for there, device in meets:
            count = count + there.astype(jnp.int32)

            @pl.when(there)
            def _():
                pl.semaphore_signal(barrier, inc=1, device_id=device, device_id_type=MESH)

        pl.semaphore_wait(barrier, count)

    def add(self, source, target, device, sends, receives):
        n = len(self.copies)
        descriptor = pltpu.make_async_remote_copy(
            src_ref=source, dst_ref=target, send_sem=self.send.at[n], recv_sem=self.recv.at[n],
            device_id=device, device_id_type=MESH,
        )
        self.copies.append((descriptor, sends, receives))
        return n

    def copy(self, direction, source, target, also=None):
        sends, receives = self.has[direction], self.has[OPPOSITE[direction]]
        if also is not None:
            sends, receives = sends & self.has[also], receives & self.has[also]
        if direction in self.ways:
            first, _, last = self.ways[direction]
            inside = jnp.logical_not(self.edge["first"] | self.edge["last"])
            sends, receives = sends & (inside | (self.x != first)), receives & (inside | (self.x != last))
        return self.add(source, target, self.target(direction), sends, receives)

    def detour(self, direction, source, buffer, target, rows=("first", "last")):
        first, relay, last = self.ways[direction]
        edge, by = (functools.reduce(jnp.logical_or, [flags[row] for row in rows]) for flags in (self.edge, self.by))
        by = by & (self.x == relay)
        return (
            self.add(source, buffer, self.at(self.away, relay), edge & (self.x == first), by),
            self.add(buffer, target, self.at(self.back, last), by, edge & (self.x == last)),
        )

    def start(self, n):
        descriptor, sends, _ = self.copies[n]
        pl.when(sends)(descriptor.start)

    def arrived(self, n, then=None):
        descriptor, _, receives = self.copies[n]

        @pl.when(receives)
        def _():
            descriptor.wait_recv()
            if then is not None:
                then()

    def finish(self):
        for descriptor, sends, _ in self.copies:
            pl.when(sends)(descriptor.wait_send)


def halo_kernel(mesh_shape, order, field, measured, ext, root, values, perm, relay, send, recv, sem):
    tile = field.shape[1]
    slots = measured.shape[0]
    blocks = tile // LANES
    loads = [
        pltpu.make_async_copy(measured.at[:, :, pl.ds(i * LANES, LANES)], values.at[:, i], sem.at[i]) for i in range(2)
    ]
    net = Exchange(mesh_shape, order, send, recv)
    inside = pl.ds(HALO, tile)
    rows = {"up": (pl.ds(0, HALO), pl.ds(HALO + tile, HALO)), "down": (pl.ds(tile - HALO, HALO), pl.ds(0, HALO))}
    column = [pl.ds(i * LANES, LANES) for i in range(blocks)]
    inner = range(1, blocks - 1)
    vertical = {}
    for i in (0, blocks - 1, *inner):
        for direction, (part, place) in rows.items():
            vertical[direction, i] = net.copy(direction, field.at[:, part, column[i]], ext.at[:, 1 + i, place, :])
    sides = [
        net.copy("left", field.at[:, :, column[0]], ext.at[:, 1 + blocks, inside, :]),
        net.copy("right", field.at[:, :, column[-1]], ext.at[:, 0, inside, :]),
    ]
    strips = []
    for k in range(0, tile, HALO):
        part, place = pl.ds(k, HALO), pl.ds(HALO + k, HALO)
        for towards, i, target in (("left", 0, 1 + blocks), ("right", blocks - 1, 0)):
            strips.append(net.detour(towards, field.at[:, part, column[i]], relay.at[:, part, :], ext.at[:, target, place, :]))
    corners, turns = [], []
    for direction, also, edge in (("down", "up", "last"), ("up", "down", "first")):
        place = rows[direction][1]
        for i, block, towards, target in ((0, 1, "left", 1 + blocks), (blocks - 1, blocks, "right", 0)):
            source, target = ext.at[:, block, place, :], ext.at[:, target, place, :]
            n = net.copy(towards, source, target, also)
            turn = net.detour(towards, source, relay.at[:, pl.ds(tile, HALO), :], target, (edge,))
            corners.append((direction, i, n, turn[0]))
            turns.append(turn)

    net.barrier()
    for first, _ in strips:
        net.start(first)
    for i in (0, blocks - 1):
        for direction in rows:
            net.start(vertical[direction, i])
    for n in sides:
        net.start(n)
    for i in inner:
        for direction in rows:
            net.start(vertical[direction, i])
    own = [pltpu.make_async_copy(field.at[:, :, column[i]], ext.at[:, 1 + i, inside, :], sem.at[2 + i]) for i in range(blocks)]
    for load in loads + own:
        load.start()

    def clear(there, blocks, first, count):
        @pl.when(jnp.logical_not(there))
        def _():
            for block in blocks:
                for part in range(2):
                    ext[part, block, first:first + count, :] = jnp.zeros((count, LANES), F32)

    has = net.has
    middle = range(1, 1 + blocks)
    clear(has["up"], middle, 0, HALO)
    clear(has["down"], middle, HALO + tile, HALO)
    for direction, block in (("left", 0), ("right", 1 + blocks)):
        clear(has[direction], (block,), HALO, tile)
        clear(has[direction] & has["up"], (block,), 0, HALO)
        clear(has[direction] & has["down"], (block,), HALO + tile, HALO)
    k = lax.broadcasted_iota(jnp.int32, (W, W), 0)
    perm[...] = (lax.broadcasted_iota(jnp.int32, (W, W), 1) == (k % 2) * H + k // 2).astype(F32).astype(BF16)
    for load in loads:
        load.wait()

    @pl.loop(0, slots)
    def _(slot):
        for half in range(2):
            x = jnp.sqrt(jnp.concatenate([values[slot, i, pl.ds(half, H, stride=2), :] for i in range(2)], axis=1))
            first = x.astype(BF16)
            x = x - first.astype(F32)
            second = x.astype(BF16)
            third = (x - second.astype(F32)).astype(BF16)
            root[slot, half * H:(half + 1) * H, :] = dot(first, perm[...]) + dot(second, perm[...]) + dot(third, perm[...])

    for load in own:
        load.wait()
    def forward(pairs):
        for first, second in pairs:
            net.arrived(first, lambda: net.start(second))

    forward(strips)
    forward(turns)
    for direction, i, n, turn in corners:
        def send():
            net.start(n)
            net.start(turn)

        net.arrived(vertical[direction, i], send)
    for n in sides:
        net.arrived(n)
    for i in inner:
        for direction in rows:
            net.arrived(vertical[direction, i])
    for _, second in strips + turns:
        net.arrived(second)
    for _, _, n, _ in corners:
        net.arrived(n)
    net.finish()


def halo_call(mesh_shape, order, field, measured):
    tile = field.shape[1]
    side = tile + 2 * HALO
    hbm = pl.BlockSpec(memory_space=pltpu.HBM)
    vmem = pl.BlockSpec(memory_space=pltpu.VMEM)
    blocks = tile // LANES
    n = 2 * blocks + 6 + 8 + 4 * (tile // HALO)
    return pl.pallas_call(
        functools.partial(halo_kernel, mesh_shape, order),
        out_shape=(
            jax.ShapeDtypeStruct((2, blocks + 3, side, LANES), F32),
            jax.ShapeDtypeStruct(measured.shape, F32),
        ),
        in_specs=[hbm, hbm],
        out_specs=(vmem, vmem),
        scratch_shapes=[
            pltpu.VMEM((measured.shape[0], 2, W, LANES), F32),
            pltpu.VMEM((W, W), BF16),
            pltpu.VMEM((2, tile + HALO, LANES), F32),
            pltpu.SemaphoreType.DMA((n,)),
            pltpu.SemaphoreType.DMA((n,)),
            pltpu.SemaphoreType.DMA((2 + blocks,)),
        ],
        compiler_params=pltpu.CompilerParams(collective_id=0, has_side_effects=True, vmem_limit_bytes=12 * 1024 * 1024),
        name="halo",
    )(pltpu.with_memory_space_constraint(field, pltpu.HBM), pltpu.with_memory_space_constraint(measured, pltpu.HBM))


def sum_kernel(mesh_shape, order, total, out, edges, from_left, from_right, from_up, from_down, send, recv):
    side = total.shape[2]
    tile = side - 2 * HALO
    blocks = tile // LANES
    net = Exchange(mesh_shape, order, send, recv)
    low, mid, high = pl.ds(0, HALO), pl.ds(HALO, tile), pl.ds(HALO + tile, HALO)
    across = {
        (direction, i): net.copy(direction, total.at[:, block, rows, :], target.at[:, rows, :])
        for i, rows in enumerate((low, high, mid))
        for direction, block, target in (("left", 0, from_right), ("right", blocks + 1, from_left))
    }
    strips, turns = [], {}
    for direction, block, target, relay in (("left", 0, from_right, from_left), ("right", blocks + 1, from_left, from_right)):
        def part(rows):
            return total.at[:, block, rows, :], relay.at[:, rows, :], target.at[:, rows, :]

        for k in range(HALO, HALO + tile, HALO):
            strips.append((direction, net.detour(direction, *part(pl.ds(k, HALO)))))
        for k, rows, edge in ((0, low, "last"), (1, high, "first")):
            turns[direction, k] = net.detour(direction, *part(rows), (edge,))
    vertical = {}
    for k, (direction, rows, target) in enumerate((("up", low, from_down), ("down", high, from_up))):
        for i in range(1, blocks - 1):
            vertical[direction, 1 + i] = net.copy(direction, total.at[:, 1 + i, rows, :], target.at[:, i])
        for i, block in ((0, 0), (1, blocks - 1)):
            vertical[direction, i] = net.copy(direction, edges.at[k, i], target.at[:, block])

    net.barrier()
    for i in (0, 1):
        for direction in ("left", "right"):
            net.start(across[direction, i])
    for first, _ in (*turns.values(), *(pair for _, pair in strips)):
        net.start(first)
    for i in range(1, blocks - 1):
        for direction in ("up", "down"):
            net.start(vertical[direction, 1 + i])
    for direction in ("left", "right"):
        net.start(across[direction, 2])

    for i in range(blocks):
        out[:, :, i * LANES:(i + 1) * LANES] = total[:, 1 + i, HALO:HALO + tile, :]
    for k, rows in enumerate((low, high)):
        for i, block in ((0, 1), (1, blocks)):
            edges[k, i] = total[:, block, rows, :]

    def forward(pairs):
        for first, second in pairs:
            net.arrived(first, lambda: net.start(second))

    half = tile // HALO // 2
    pairs = [pair for _, pair in strips]
    early, late = pairs[:half] + pairs[2 * half:3 * half], pairs[half:2 * half] + pairs[3 * half:]
    forward(turns.values())
    forward(early)
    for k, (rows, direction) in enumerate(((low, "up"), (high, "down"))):
        for i, towards, source in ((0, "right", from_left), (1, "left", from_right)):
            def add():
                edges[k, i] = edges[k, i] + source[:, rows, :]

            net.arrived(across[towards, k], add)
            net.arrived(turns[towards, k][1], add)
            net.start(vertical[direction, i])

    forward(late)
    for i, towards, source in ((0, "right", from_left), (blocks - 1, "left", from_right)):
        waits = []

        def add():
            columns = slice(i * LANES, (i + 1) * LANES)
            out[:, :, columns] = out[:, :, columns] + source[:, mid, :]

        net.arrived(across[towards, 2], add)
        for direction, (_, second) in strips:
            if direction == towards:
                waits.append(second)
        last = waits.pop()
        for second in waits:
            net.arrived(second)
        net.arrived(last, add)

    for i, part in (*((1 + part, part) for part in range(1, blocks - 1)), (0, 0), (1, blocks - 1)):
        for towards, first, source in (("down", 0, from_up), ("up", tile - HALO, from_down)):
            def add():
                place = (slice(None), slice(first, first + HALO), slice(part * LANES, (part + 1) * LANES))
                out[place] = out[place] + source[:, part]

            net.arrived(vertical[towards, i], add)
    net.finish()


def sum_call(mesh_shape, order, total):
    side = total.shape[2]
    tile = side - 2 * HALO
    blocks = tile // LANES
    n = 6 + 2 * blocks + 8 + 4 * (tile // HALO)
    vmem = pl.BlockSpec(memory_space=pltpu.VMEM)
    return pl.pallas_call(
        functools.partial(sum_kernel, mesh_shape, order),
        out_shape=jax.ShapeDtypeStruct((2, tile, tile), F32),
        in_specs=[vmem],
        out_specs=vmem,
        scratch_shapes=[
            pltpu.VMEM((2, 2, 2, HALO, LANES), F32),
            pltpu.VMEM((2, side, LANES), F32),
            pltpu.VMEM((2, side, LANES), F32),
            pltpu.VMEM((2, blocks, HALO, LANES), F32),
            pltpu.VMEM((2, blocks, HALO, LANES), F32),
            pltpu.SemaphoreType.DMA((n,)),
            pltpu.SemaphoreType.DMA((n,)),
        ],
        compiler_params=pltpu.CompilerParams(collective_id=1, has_side_effects=True, vmem_limit_bytes=16 * 1024 * 1024),
        name="sums",
    )(total)


def frames_kernel(
    spots, count, tables, probe, root, ext,
    total,
    patch, stage2, wave, stage3, stage4, grad,
):
    modes = probe.shape[0]

    @pl.loop(0, total.shape[2] // 16)
    def _(i):
        total[:, :, pl.ds(pl.multiple_of(i * 16, 16), 16), :] = jnp.zeros((2, total.shape[1], 16, LANES), F32)

    lane = lax.broadcasted_iota(jnp.int32, (W, LANES), 1)

    @pl.loop(0, count[0, 0])
    def _(slot):
        row = spots[0, 0, 0, slot]
        column = spots[0, 0, 1, slot]
        block = column // LANES
        shift = column - block * LANES
        back = lax.rem(LANES - shift, LANES)
        keep = lane < LANES - shift
        for part in range(2):
            rolled = []
            for i in range(3):
                x = ext[part, block + i, pl.ds(row, W), :]
                rolled.append(pltpu.roll(x, back, axis=1))
            for i in range(2):
                patch[part, :, i * LANES:(i + 1) * LANES] = jnp.where(keep, rolled[i], rolled[i + 1])

        step = 64
        for first in range(0, H, step):
            even, odd = [], []
            for m in range(modes):
                for half in range(2):
                    rows = pl.ds(half * H + first, step)
                    pr, pi = probe[m, 0, rows, :], probe[m, 1, rows, :]
                    xr, xi = patch[0, rows, :], patch[1, rows, :]
                    re = pr * xr - pi * xi
                    im = pr * xi + pi * xr
                    even.append(jnp.concatenate([re[:, :H] + re[:, H:], im[:, :H] + im[:, H:]], axis=1))
                    odd.append(jnp.concatenate([re[:, :H] - re[:, H:], im[:, :H] - im[:, H:]], axis=1))
            even = dot(jnp.concatenate(even, axis=0).astype(BF16), tables[0])
            odd = dot(jnp.concatenate(odd, axis=0).astype(BF16), tables[1])
            for m in range(modes):
                for n, h in enumerate((even, odd)):
                    low = h[(2 * m) * step:(2 * m + 1) * step]
                    high = h[(2 * m + 1) * step:(2 * m + 2) * step]
                    plus, minus = (low + high).astype(BF16), (low - high).astype(BF16)
                    for part in range(2):
                        rows = pl.ds(part * H + first, step)
                        columns = slice(part * H, (part + 1) * H)
                        stage2[m, 0, rows, n * H:(n + 1) * H] = plus[:, columns]
                        stage2[m, 1, rows, n * H:(n + 1) * H] = minus[:, columns]

        for n in range(2):
            for m in range(modes):
                wave[m, n] = dot(tables[2 + n], stage2[m, n])
            for first in range(0, H, 16):
                res = [wave[m, n, pl.ds(first, 16), :] for m in range(modes)]
                ims = [wave[m, n, pl.ds(H + first, 16), :] for m in range(modes)]
                inten = sum(x * x for x in res[1:] + ims) + res[0] * res[0]
                factor = 1.0 - root[slot, pl.ds(n * H + first, 16), :] * lax.rsqrt(inten + 1.0)
                for m in range(modes):
                    stage3[m, n, pl.ds(first, 16), :] = (factor * res[m]).astype(BF16)
                    stage3[m, n, pl.ds(H + first, 16), :] = (factor * ims[m]).astype(BF16)

        for m in range(modes):
            even = dot(tables[0], stage3[m, 0])
            odd = dot(tables[1], stage3[m, 1])
            plus, minus = (even + odd).astype(BF16), (even - odd).astype(BF16)
            for half, x in enumerate((plus, minus)):
                for part in range(2):
                    for n in range(2):
                        stage4[n, m, half * H:(half + 1) * H, part * H:(part + 1) * H] = x[part * H:(part + 1) * H, n * H:(n + 1) * H]

        step = 128
        for first in range(0, W, step):
            rows = pl.ds(first, step)
            even = dot(stage4[0, :, rows, :].reshape(modes * step, W), tables[2])
            odd = dot(stage4[1, :, rows, :].reshape(modes * step, W), tables[3])
            plus, minus = even + odd, even - odd
            for half, x in enumerate((plus, minus)):
                columns = slice(half * H, (half + 1) * H)
                gr = gi = None
                for m in range(modes):
                    pr, pi = probe[m, 0, rows, columns], probe[m, 1, rows, columns]
                    cr, ci = x[m * step:(m + 1) * step, :H], x[m * step:(m + 1) * step, H:]
                    re, im = pr * cr + pi * ci, pr * ci - pi * cr
                    gr, gi = (re, im) if gr is None else (gr + re, gi + im)
                grad[0, rows, columns] = gr
                grad[1, rows, columns] = gi

        moved = lane >= shift
        for part in range(2):
            left = pltpu.roll(grad[part, :, 0:LANES], shift, axis=1)
            right = pltpu.roll(grad[part, :, LANES:2 * LANES], shift, axis=1)
            zero = jnp.zeros_like(left)
            pieces = (jnp.where(moved, left, zero), jnp.where(moved, right, left), jnp.where(moved, zero, right))
            for i, piece in enumerate(pieces):
                where = (part, block + i, pl.ds(row, W), slice(None))
                total[where] = total[where] + piece


def frames_call(spots, count, probe, root, ext):
    modes = probe.shape[0]
    smem = pl.BlockSpec(memory_space=pltpu.SMEM)
    vmem = pl.BlockSpec(memory_space=pltpu.VMEM)
    return pl.pallas_call(
        frames_kernel,
        out_shape=jax.ShapeDtypeStruct(ext.shape, F32),
        in_specs=[smem, smem, vmem, vmem, vmem, vmem],
        out_specs=vmem,
        scratch_shapes=[
            pltpu.VMEM((2, W, W), F32),
            pltpu.VMEM((modes, 2, W, W), BF16),
            pltpu.VMEM((modes, 2, W, W), F32),
            pltpu.VMEM((modes, 2, W, W), BF16),
            pltpu.VMEM((2, modes, W, W), BF16),
            pltpu.VMEM((2, W, W), F32),
        ],
        compiler_params=pltpu.CompilerParams(vmem_limit_bytes=28 * 1024 * 1024),
        name="frames",
    )(spots, count, jnp.asarray(dft_tables()), probe, root, ext)


def body(mesh_shape, order, object_field, probe, positions, frame_count, measured):
    ext, root = halo_call(mesh_shape, order, object_field, measured[0, 0])
    total = frames_call(jnp.swapaxes(positions, 2, 3), frame_count, probe, root, ext)
    return sum_call(mesh_shape, order, total)


def solution(mesh):
    mesh_shape = (mesh.shape["gy"], mesh.shape["gx"])
    return jax.shard_map(
        functools.partial(body, mesh_shape, tuple(mesh.axis_names)),
        mesh=mesh,
        in_specs=(
            P(None, "gy", "gx"),
            P(),
            P("gy", "gx", None, None),
            P("gy", "gx"),
            P("gy", "gx", None, None, None),
        ),
        out_specs=P(None, "gy", "gx"),
        check_vma=False,
    )
```

```python
import functools
import math

import jax
import jax.numpy as jnp
import ml_dtypes
import numpy as np
from jax import lax
from jax.experimental import pallas as pl
from jax.experimental.pallas import tpu as pltpu
from jax.sharding import PartitionSpec as P

HALO = 128
W = 256
H = 128
LANES = 128
F32 = jnp.float32
BF16 = jnp.bfloat16
MESH = pl.DeviceIdType.MESH


def dft_tables():
    j = np.arange(H)[:, None]
    k = np.arange(H)[None, :]
    tables = []
    for odd in (0, 1):
        phase = 2.0 * math.pi / W * np.mod(j * (2 * k + odd), W)
        cosine = np.cos(phase) / math.sqrt(W)
        sine = np.sin(phase) / math.sqrt(W)
        tables.append(np.block([[cosine, -sine], [sine, cosine]]))
    tables += [tables[0].T, tables[1].T]
    return np.stack(tables).astype(ml_dtypes.bfloat16)


def dot(a, b):
    return jnp.dot(a, b, preferred_element_type=F32)


def neighbours(mesh_shape):
    ny, nx = mesh_shape
    y, x = lax.axis_index("gy"), lax.axis_index("gx")
    return y, x, dict(up=y > 0, down=y < ny - 1, left=x > 0, right=x < nx - 1)


def device(direction, y, x, mesh_shape):
    ny, nx = mesh_shape
    return {
        "up": (jnp.maximum(y - 1, 0), x),
        "down": (jnp.minimum(y + 1, ny - 1), x),
        "left": (y, jnp.maximum(x - 1, 0)),
        "right": (y, jnp.minimum(x + 1, nx - 1)),
    }[direction]


OPPOSITE = dict(up="down", down="up", left="right", right="left")


class Exchange:
    def __init__(self, mesh_shape, order, send, recv):
        self.shape, self.send, self.recv = mesh_shape, send, recv
        self.order = order
        self.y, self.x, self.has = neighbours(mesh_shape)
        ny = mesh_shape[0]
        first, above, below, last = 0, ny // 2 - 1, ny // 2, ny - 1
        self.edge = {"first": self.y == first, "last": self.y == last}
        self.by = {"first": self.y == below, "last": self.y == above}
        self.away = jnp.where(self.edge["first"], below, above)
        self.back = jnp.where(self.by["first"], first, last)
        middle = mesh_shape[1] // 2
        self.ways = {"right": (middle - 1, mesh_shape[1] - 1, middle), "left": (middle, 0, middle - 1)}
        self.copies = []

    def at(self, y, x):
        at = {"gy": y, "gx": x}
        return tuple(at[name] for name in self.order)

    def target(self, direction):
        return self.at(*device(direction, self.y, self.x, self.shape))

    def barrier(self):
        barrier = pltpu.get_barrier_semaphore()
        count = 0
        meets = [(there, self.target(direction)) for direction, there in self.has.items()]
        edge, by = self.edge["first"] | self.edge["last"], self.by["first"] | self.by["last"]
        for source, relay, target in self.ways.values():
            for column in (source, target):
                meets.append((edge & (self.x == column), self.at(self.away, relay)))
                meets.append((by & (self.x == relay), self.at(self.back, column)))
        for there, device in meets:
            count = count + there.astype(jnp.int32)

            @pl.when(there)
            def _():
                pl.semaphore_signal(barrier, inc=1, device_id=device, device_id_type=MESH)

        pl.semaphore_wait(barrier, count)

    def add(self, source, target, device, sends, receives):
        n = len(self.copies)
        descriptor = pltpu.make_async_remote_copy(
            src_ref=source, dst_ref=target, send_sem=self.send.at[n], recv_sem=self.recv.at[n],
            device_id=device, device_id_type=MESH,
        )
        self.copies.append((descriptor, sends, receives))
        return n

    def copy(self, direction, source, target, also=None):
        sends, receives = self.has[direction], self.has[OPPOSITE[direction]]
        if also is not None:
            sends, receives = sends & self.has[also], receives & self.has[also]
        if direction in self.ways:
            first, _, last = self.ways[direction]
            inside = jnp.logical_not(self.edge["first"] | self.edge["last"])
            sends, receives = sends & (inside | (self.x != first)), receives & (inside | (self.x != last))
        return self.add(source, target, self.target(direction), sends, receives)

    def detour(self, direction, source, buffer, target, rows=("first", "last")):
        first, relay, last = self.ways[direction]
        edge, by = (functools.reduce(jnp.logical_or, [flags[row] for row in rows]) for flags in (self.edge, self.by))
        by = by & (self.x == relay)
        return (
            self.add(source, buffer, self.at(self.away, relay), edge & (self.x == first), by),
            self.add(buffer, target, self.at(self.back, last), by, edge & (self.x == last)),
        )

    def start(self, n):
        descriptor, sends, _ = self.copies[n]
        pl.when(sends)(descriptor.start)

    def arrived(self, n, then=None, only=None):
        descriptor, _, receives = self.copies[n]
        receives = receives if only is None else receives & only

        @pl.when(receives)
        def _():
            descriptor.wait_recv()
            if then is not None:
                then()

    def finish(self):
        for descriptor, sends, _ in self.copies:
            pl.when(sends)(descriptor.wait_send)


def halo_kernel(mesh_shape, order, field, measured, ext, root, values, perm, relay, send, recv, sem):
    tile = field.shape[1]
    slots = measured.shape[0]
    blocks = tile // LANES
    loads = [
        pltpu.make_async_copy(measured.at[:, :, pl.ds(i * LANES, LANES)], values.at[:, i], sem.at[i]) for i in range(2)
    ]
    net = Exchange(mesh_shape, order, send, recv)
    inside = pl.ds(HALO, tile)
    rows = {"up": (pl.ds(0, HALO), pl.ds(HALO + tile, HALO)), "down": (pl.ds(tile - HALO, HALO), pl.ds(0, HALO))}
    column = [pl.ds(i * LANES, LANES) for i in range(blocks)]
    inner = range(1, blocks - 1)
    vertical = {}
    for i in (0, blocks - 1, *inner):
        for direction, (part, place) in rows.items():
            vertical[direction, i] = net.copy(direction, field.at[:, part, column[i]], ext.at[:, 1 + i, place, :])
    sides = [
        net.copy("left", field.at[:, :, column[0]], ext.at[:, 1 + blocks, inside, :]),
        net.copy("right", field.at[:, :, column[-1]], ext.at[:, 0, inside, :]),
    ]
    strips = []
    for k in range(0, tile, HALO):
        part, place = pl.ds(k, HALO), pl.ds(HALO + k, HALO)
        for towards, i, target in (("left", 0, 1 + blocks), ("right", blocks - 1, 0)):
            strips.append(net.detour(towards, field.at[:, part, column[i]], relay.at[:, part, :], ext.at[:, target, place, :]))
    corners, turns = [], []
    for direction, also, edge in (("down", "up", "last"), ("up", "down", "first")):
        place = rows[direction][1]
        for i, block, towards, target in ((0, 1, "left", 1 + blocks), (blocks - 1, blocks, "right", 0)):
            source, target = ext.at[:, block, place, :], ext.at[:, target, place, :]
            n = net.copy(towards, source, target, also)
            turn = net.detour(towards, source, relay.at[:, pl.ds(tile, HALO), :], target, (edge,))
            corners.append((direction, i, n, turn[0]))
            turns.append(turn)

    net.barrier()
    for first, _ in strips:
        net.start(first)
    for i in (0, blocks - 1):
        for direction in rows:
            net.start(vertical[direction, i])
    for n in sides:
        net.start(n)
    for i in inner:
        for direction in rows:
            net.start(vertical[direction, i])
    own = [pltpu.make_async_copy(field.at[:, :, column[i]], ext.at[:, 1 + i, inside, :], sem.at[2 + i]) for i in range(blocks)]
    for load in loads + own:
        load.start()

    def clear(there, blocks, first, count):
        @pl.when(jnp.logical_not(there))
        def _():
            for block in blocks:
                for part in range(2):
                    ext[part, block, first:first + count, :] = jnp.zeros((count, LANES), F32)

    has = net.has
    middle = range(1, 1 + blocks)
    clear(has["up"], middle, 0, HALO)
    clear(has["down"], middle, HALO + tile, HALO)
    for direction, block in (("left", 0), ("right", 1 + blocks)):
        clear(has[direction], (block,), HALO, tile)
        clear(has[direction] & has["up"], (block,), 0, HALO)
        clear(has[direction] & has["down"], (block,), HALO + tile, HALO)
    k = lax.broadcasted_iota(jnp.int32, (W, W), 0)
    perm[...] = (lax.broadcasted_iota(jnp.int32, (W, W), 1) == (k % 2) * H + k // 2).astype(F32).astype(BF16)
    for load in loads:
        load.wait()

    @pl.loop(0, slots)
    def _(slot):
        for half in range(2):
            x = jnp.sqrt(jnp.concatenate([values[slot, i, pl.ds(half, H, stride=2), :] for i in range(2)], axis=1))
            first = x.astype(BF16)
            x = x - first.astype(F32)
            second = x.astype(BF16)
            third = (x - second.astype(F32)).astype(BF16)
            root[slot, half * H:(half + 1) * H, :] = dot(first, perm[...]) + dot(second, perm[...]) + dot(third, perm[...])

    for load in own:
        load.wait()
    def forward(pairs):
        for first, second in pairs:
            net.arrived(first, lambda: net.start(second))

    def relay_corners(entries, only=None):
        for direction, i, n, turn in entries:
            def send():
                net.start(n)
                net.start(turn)

            net.arrived(vertical[direction, i], send, only)

    forward(strips)
    lower = net.by["first"]
    relay_corners(corners[2:], lower)
    relay_corners(corners[:2])
    forward(turns)
    relay_corners(corners[2:], jnp.logical_not(lower))
    for n in sides:
        net.arrived(n)
    for i in inner:
        for direction in rows:
            net.arrived(vertical[direction, i])
    for _, second in strips + turns:
        net.arrived(second)
    for _, _, n, _ in corners:
        net.arrived(n)
    net.finish()


def halo_call(mesh_shape, order, field, measured):
    tile = field.shape[1]
    side = tile + 2 * HALO
    hbm = pl.BlockSpec(memory_space=pltpu.HBM)
    vmem = pl.BlockSpec(memory_space=pltpu.VMEM)
    blocks = tile // LANES
    n = 2 * blocks + 6 + 8 + 4 * (tile // HALO)
    return pl.pallas_call(
        functools.partial(halo_kernel, mesh_shape, order),
        out_shape=(
            jax.ShapeDtypeStruct((2, blocks + 3, side, LANES), F32),
            jax.ShapeDtypeStruct(measured.shape, F32),
        ),
        in_specs=[hbm, hbm],
        out_specs=(vmem, vmem),
        scratch_shapes=[
            pltpu.VMEM((measured.shape[0], 2, W, LANES), F32),
            pltpu.VMEM((W, W), BF16),
            pltpu.VMEM((2, tile + HALO, LANES), F32),
            pltpu.SemaphoreType.DMA((n,)),
            pltpu.SemaphoreType.DMA((n,)),
            pltpu.SemaphoreType.DMA((2 + blocks,)),
        ],
        compiler_params=pltpu.CompilerParams(collective_id=0, has_side_effects=True, vmem_limit_bytes=12 * 1024 * 1024),
        name="halo",
    )(pltpu.with_memory_space_constraint(field, pltpu.HBM), pltpu.with_memory_space_constraint(measured, pltpu.HBM))


def sum_kernel(mesh_shape, order, total, out, edges, from_left, from_right, from_up, from_down, send, recv):
    side = total.shape[2]
    tile = side - 2 * HALO
    blocks = tile // LANES
    net = Exchange(mesh_shape, order, send, recv)
    low, mid, high = pl.ds(0, HALO), pl.ds(HALO, tile), pl.ds(HALO + tile, HALO)
    across = {
        (direction, i): net.copy(direction, total.at[:, block, rows, :], target.at[:, rows, :])
        for i, rows in enumerate((low, high, mid))
        for direction, block, target in (("left", 0, from_right), ("right", blocks + 1, from_left))
    }
    strips, turns = [], {}
    for direction, block, target, relay in (("left", 0, from_right, from_left), ("right", blocks + 1, from_left, from_right)):
        def part(rows):
            return total.at[:, block, rows, :], relay.at[:, rows, :], target.at[:, rows, :]

        for k in range(HALO, HALO + tile, HALO):
            strips.append((direction, net.detour(direction, *part(pl.ds(k, HALO)))))
        for k, rows, edge in ((0, low, "last"), (1, high, "first")):
            turns[direction, k] = net.detour(direction, *part(rows), (edge,))
    vertical = {}
    for k, (direction, rows, target) in enumerate((("up", low, from_down), ("down", high, from_up))):
        for i in range(1, blocks - 1):
            vertical[direction, 1 + i] = net.copy(direction, total.at[:, 1 + i, rows, :], target.at[:, i])
        for i, block in ((0, 0), (1, blocks - 1)):
            vertical[direction, i] = net.copy(direction, edges.at[k, i], target.at[:, block])

    net.barrier()
    for i in (0, 1):
        for direction in ("left", "right"):
            net.start(across[direction, i])
    for first, _ in (*turns.values(), *(pair for _, pair in strips)):
        net.start(first)
    for i in range(1, blocks - 1):
        for direction in ("up", "down"):
            net.start(vertical[direction, 1 + i])
    for direction in ("left", "right"):
        net.start(across[direction, 2])

    for i in range(blocks):
        out[:, :, i * LANES:(i + 1) * LANES] = total[:, 1 + i, HALO:HALO + tile, :]
    for k, rows in enumerate((low, high)):
        for i, block in ((0, 1), (1, blocks)):
            edges[k, i] = total[:, block, rows, :]

    def forward(pairs):
        for first, second in pairs:
            net.arrived(first, lambda: net.start(second))

    half = tile // HALO // 2
    pairs = [pair for _, pair in strips]
    early, late = pairs[:half] + pairs[2 * half:3 * half], pairs[half:2 * half] + pairs[3 * half:]
    forward(turns.values())
    forward(early)
    for k, (rows, direction) in enumerate(((low, "up"), (high, "down"))):
        for i, towards, source in ((0, "right", from_left), (1, "left", from_right)):
            def add():
                edges[k, i] = edges[k, i] + source[:, rows, :]

            net.arrived(across[towards, k], add)
            net.arrived(turns[towards, k][1], add)
            net.start(vertical[direction, i])

    forward(late)
    for i, towards, source in ((0, "right", from_left), (blocks - 1, "left", from_right)):
        waits = []

        def add():
            columns = slice(i * LANES, (i + 1) * LANES)
            out[:, :, columns] = out[:, :, columns] + source[:, mid, :]

        net.arrived(across[towards, 2], add)
        for direction, (_, second) in strips:
            if direction == towards:
                waits.append(second)
        last = waits.pop()
        for second in waits:
            net.arrived(second)
        net.arrived(last, add)

    for i, part in (*((1 + part, part) for part in range(1, blocks - 1)), (0, 0), (1, blocks - 1)):
        for towards, first, source in (("down", 0, from_up), ("up", tile - HALO, from_down)):
            def add():
                place = (slice(None), slice(first, first + HALO), slice(part * LANES, (part + 1) * LANES))
                out[place] = out[place] + source[:, part]

            net.arrived(vertical[towards, i], add)
    net.finish()


def sum_call(mesh_shape, order, total):
    side = total.shape[2]
    tile = side - 2 * HALO
    blocks = tile // LANES
    n = 6 + 2 * blocks + 8 + 4 * (tile // HALO)
    vmem = pl.BlockSpec(memory_space=pltpu.VMEM)
    return pl.pallas_call(
        functools.partial(sum_kernel, mesh_shape, order),
        out_shape=jax.ShapeDtypeStruct((2, tile, tile), F32),
        in_specs=[vmem],
        out_specs=vmem,
        scratch_shapes=[
            pltpu.VMEM((2, 2, 2, HALO, LANES), F32),
            pltpu.VMEM((2, side, LANES), F32),
            pltpu.VMEM((2, side, LANES), F32),
            pltpu.VMEM((2, blocks, HALO, LANES), F32),
            pltpu.VMEM((2, blocks, HALO, LANES), F32),
            pltpu.SemaphoreType.DMA((n,)),
            pltpu.SemaphoreType.DMA((n,)),
        ],
        compiler_params=pltpu.CompilerParams(collective_id=1, has_side_effects=True, vmem_limit_bytes=16 * 1024 * 1024),
        name="sums",
    )(total)


def frames_kernel(
    spots, count, tables, probe, root, ext,
    total,
    patch, stage2, wave, stage3, stage4, grad,
):
    modes = probe.shape[0]

    @pl.loop(0, total.shape[2] // 16)
    def _(i):
        total[:, :, pl.ds(pl.multiple_of(i * 16, 16), 16), :] = jnp.zeros((2, total.shape[1], 16, LANES), F32)

    lane = lax.broadcasted_iota(jnp.int32, (W, LANES), 1)

    @pl.loop(0, count[0, 0])
    def _(slot):
        row = spots[0, 0, 0, slot]
        column = spots[0, 0, 1, slot]
        block = column // LANES
        shift = column - block * LANES
        back = lax.rem(LANES - shift, LANES)
        keep = lane < LANES - shift
        for part in range(2):
            rolled = []
            for i in range(3):
                x = ext[part, block + i, pl.ds(row, W), :]
                rolled.append(pltpu.roll(x, back, axis=1))
            for i in range(2):
                patch[part, :, i * LANES:(i + 1) * LANES] = jnp.where(keep, rolled[i], rolled[i + 1])

        step = 64
        for first in range(0, H, step):
            even, odd = [], []
            for m in range(modes):
                for half in range(2):
                    rows = pl.ds(half * H + first, step)
                    pr, pi = probe[m, 0, rows, :], probe[m, 1, rows, :]
                    xr, xi = patch[0, rows, :], patch[1, rows, :]
                    re = pr * xr - pi * xi
                    im = pr * xi + pi * xr
                    even.append(jnp.concatenate([re[:, :H] + re[:, H:], im[:, :H] + im[:, H:]], axis=1))
                    odd.append(jnp.concatenate([re[:, :H] - re[:, H:], im[:, :H] - im[:, H:]], axis=1))
            even = dot(jnp.concatenate(even, axis=0).astype(BF16), tables[0])
            odd = dot(jnp.concatenate(odd, axis=0).astype(BF16), tables[1])
            for m in range(modes):
                for n, h in enumerate((even, odd)):
                    low = h[(2 * m) * step:(2 * m + 1) * step]
                    high = h[(2 * m + 1) * step:(2 * m + 2) * step]
                    plus, minus = (low + high).astype(BF16), (low - high).astype(BF16)
                    for part in range(2):
                        rows = pl.ds(part * H + first, step)
                        columns = slice(part * H, (part + 1) * H)
                        stage2[m, 0, rows, n * H:(n + 1) * H] = plus[:, columns]
                        stage2[m, 1, rows, n * H:(n + 1) * H] = minus[:, columns]

        for n in range(2):
            for m in range(modes):
                wave[m, n] = dot(tables[2 + n], stage2[m, n])
            for first in range(0, H, 16):
                res = [wave[m, n, pl.ds(first, 16), :] for m in range(modes)]
                ims = [wave[m, n, pl.ds(H + first, 16), :] for m in range(modes)]
                inten = sum(x * x for x in res[1:] + ims) + res[0] * res[0]
                factor = 1.0 - root[slot, pl.ds(n * H + first, 16), :] * lax.rsqrt(inten + 1.0)
                for m in range(modes):
                    stage3[m, n, pl.ds(first, 16), :] = (factor * res[m]).astype(BF16)
                    stage3[m, n, pl.ds(H + first, 16), :] = (factor * ims[m]).astype(BF16)

        for m in range(modes):
            even = dot(tables[0], stage3[m, 0])
            odd = dot(tables[1], stage3[m, 1])
            plus, minus = (even + odd).astype(BF16), (even - odd).astype(BF16)
            for half, x in enumerate((plus, minus)):
                for part in range(2):
                    for n in range(2):
                        stage4[n, m, half * H:(half + 1) * H, part * H:(part + 1) * H] = x[part * H:(part + 1) * H, n * H:(n + 1) * H]

        step = 128
        for first in range(0, W, step):
            rows = pl.ds(first, step)
            even = dot(stage4[0, :, rows, :].reshape(modes * step, W), tables[2])
            odd = dot(stage4[1, :, rows, :].reshape(modes * step, W), tables[3])
            plus, minus = even + odd, even - odd
            for half, x in enumerate((plus, minus)):
                columns = slice(half * H, (half + 1) * H)
                gr = gi = None
                for m in range(modes):
                    pr, pi = probe[m, 0, rows, columns], probe[m, 1, rows, columns]
                    cr, ci = x[m * step:(m + 1) * step, :H], x[m * step:(m + 1) * step, H:]
                    re, im = pr * cr + pi * ci, pr * ci - pi * cr
                    gr, gi = (re, im) if gr is None else (gr + re, gi + im)
                grad[0, rows, columns] = gr
                grad[1, rows, columns] = gi

        moved = lane >= shift
        for part in range(2):
            left = pltpu.roll(grad[part, :, 0:LANES], shift, axis=1)
            right = pltpu.roll(grad[part, :, LANES:2 * LANES], shift, axis=1)
            zero = jnp.zeros_like(left)
            pieces = (jnp.where(moved, left, zero), jnp.where(moved, right, left), jnp.where(moved, zero, right))
            for i, piece in enumerate(pieces):
                where = (part, block + i, pl.ds(row, W), slice(None))
                total[where] = total[where] + piece


def frames_call(spots, count, probe, root, ext):
    modes = probe.shape[0]
    smem = pl.BlockSpec(memory_space=pltpu.SMEM)
    vmem = pl.BlockSpec(memory_space=pltpu.VMEM)
    return pl.pallas_call(
        frames_kernel,
        out_shape=jax.ShapeDtypeStruct(ext.shape, F32),
        in_specs=[smem, smem, vmem, vmem, vmem, vmem],
        out_specs=vmem,
        scratch_shapes=[
            pltpu.VMEM((2, W, W), F32),
            pltpu.VMEM((modes, 2, W, W), BF16),
            pltpu.VMEM((modes, 2, W, W), F32),
            pltpu.VMEM((modes, 2, W, W), BF16),
            pltpu.VMEM((2, modes, W, W), BF16),
            pltpu.VMEM((2, W, W), F32),
        ],
        compiler_params=pltpu.CompilerParams(vmem_limit_bytes=28 * 1024 * 1024),
        name="frames",
    )(spots, count, jnp.asarray(dft_tables()), probe, root, ext)


def body(mesh_shape, order, object_field, probe, positions, frame_count, measured):
    ext, root = halo_call(mesh_shape, order, object_field, measured[0, 0])
    total = frames_call(jnp.swapaxes(positions, 2, 3), frame_count, probe, root, ext)
    return sum_call(mesh_shape, order, total)


def solution(mesh):
    mesh_shape = (mesh.shape["gy"], mesh.shape["gx"])
    return jax.shard_map(
        functools.partial(body, mesh_shape, tuple(mesh.axis_names)),
        mesh=mesh,
        in_specs=(
            P(None, "gy", "gx"),
            P(),
            P("gy", "gx", None, None),
            P("gy", "gx"),
            P("gy", "gx", None, None, None),
        ),
        out_specs=P(None, "gy", "gx"),
        check_vma=False,
    )
```
